32 devices in a mesh: tm: 4 (over y, core), space: 8 (over z, x).
Axes of the slice: x: 2, y: 2, z: 4, core: 2. Of those that a mesh axis runs over, the one named last changes fastest.
Arguments:
- initial: float32 [4, 128, 8192], P('tm', None, 'space'), may hold values from -324 to 324
- rhs: float32 [4, 128, 8192], P('tm', None, 'space'), may hold values from -324 to 324
- coef: float32 [8192], P('space'), may hold values from 0.5 to 4
- stiffness: float32 [128, 128], replicated, may hold values from -0.5 to 0.5
- block_inverse: float32 [128, 128], replicated, may hold values from -0.5 to 0.5
- face_proj: float32 [192, 128], replicated, may hold values from -0.5 to 0.5
- lift: float32 [128, 192], replicated, may hold values from -0.4375 to 0.4375
- time_lift: float32 [128, 64], replicated, may hold values from -0.75 to 0.75
- neighbour: int32 [6, 8192], P(None, 'space'), may hold values from 0 to 6399, as said below
- boundary: int32 [6, 8192], P(None, 'space'), may hold values from 0 to 1, as said below
- send_list: int32 [2048], P('space'), may hold values from 0 to 2047, as said below
Outputs:
- smoothed: float32 [4, 128, 8192], P('tm', None, 'space')
- indicator: float32 [4, 8192], P('tm', 'space')
- estimate: float32 [1], replicated
The draws below stay inside these ranges and needn't reach their ends.
Inputs may be any that keep to these rules, and one draw needn't show every extreme that they name: `neighbour`: the elements form a structured hexahedral grid numbered in a random order inside each partition; partition p holds 8 element layers and meets partitions p - 1 and p + 1 across 128 faces each, listed in the same order on both sides. Interior faces point to the opposite face of the neighbouring element; faces toward another partition point to columns 6144 and above; boundary faces may point anywhere. `boundary`: marks the outer faces of the whole grid. `send_list`: the first 128 entries of a partition list its faces facing the lower partition, the next 128 those facing the upper one, as columns of its own pool below 2048.
All inputs are finite; a program needn't handle non-finite values.
Results may differ from the reference program's by a relative error of at most 0.000059.
Values sent between devices are 32-bit elements; how exact they have to be, the bound alone decides.
No kernel may reach another device: no remote copies, remote signals or barrier semaphores. Data moves between devices by JAX's collectives and lax.ppermute only.
A program may use at most 64 MiB of HBM per device.

```python
import math
import jax
import jax.numpy as jnp
from jax import lax

DOFS = 128
SDOFS = 64
FDOFS = 32
GX = 8
GY = 8
GZ = 16
E_DEV = 1024
NB = 128
ELEMS = 8192
SLABS = 4


def slot_order(sub_key):
    middle = 1 + jax.random.permutation(sub_key, E_DEV - 2)
    return jnp.concatenate([jnp.zeros((1,), jnp.int32), middle.astype(jnp.int32), jnp.full((1,), E_DEV - 1, jnp.int32)])


def mesh_tables(key):
    partitions = ELEMS // E_DEV
    layer_size = GY * GZ
    slot_keys = jax.random.split(jax.random.fold_in(key, 101), partitions)
    slot_of = jax.vmap(slot_order)(slot_keys).astype(jnp.int32)
    cell_ids = jnp.arange(E_DEV, dtype=jnp.int32)
    coord_x = cell_ids // layer_size
    coord_y = cell_ids // GZ % GY
    coord_z = cell_ids % GZ
    lateral = cell_ids % layer_size
    part_ids = jnp.arange(partitions, dtype=jnp.int32)[:, None]
    columns = []
    walls = []
    for face_id in range(6):
        direction = face_id // 2
        offset = 2 * (face_id % 2) - 1
        next_x = coord_x + (offset if direction == 0 else 0)
        next_y = coord_y + (offset if direction == 1 else 0)
        next_z = coord_z + (offset if direction == 2 else 0)
        inside = (next_x >= 0) & (next_x < GX) & (next_y >= 0) & (next_y < GY) & (next_z >= 0) & (next_z < GZ)
        next_cell = (jnp.clip(next_x, 0, GX - 1) * GY + jnp.clip(next_y, 0, GY - 1)) * GZ + jnp.clip(next_z, 0, GZ - 1)
        local_col = (face_id ^ 1) * E_DEV + slot_of[:, next_cell]
        if direction == 0:
            remote = 6 * E_DEV + face_id % 2 * layer_size + lateral
            column = jnp.where(inside[None, :], local_col, remote[None, :])
            end_part = 0 if face_id == 0 else partitions - 1
            is_wall = jnp.logical_not(inside)[None, :] & (part_ids == end_part)
        else:
            column = jnp.where(inside[None, :], local_col, 0)
            is_wall = jnp.broadcast_to(jnp.logical_not(inside)[None, :], (partitions, E_DEV))
        columns.append(column.astype(jnp.int32))
        walls.append(is_wall.astype(jnp.int32))

    def place(values_row, slot_row):
        return jnp.zeros_like(values_row).at[:, slot_row].set(values_row)
    placed_cols = jax.vmap(place)(jnp.stack(columns, axis=1), slot_of)
    placed_walls = jax.vmap(place)(jnp.stack(walls, axis=1), slot_of)
    neighbour = placed_cols.transpose(1, 0, 2).reshape(6, ELEMS)
    boundary = placed_walls.transpose(1, 0, 2).reshape(6, ELEMS)
    lower_list = slot_of[:, :layer_size]
    upper_list = E_DEV + slot_of[:, (GX - 1) * layer_size:]
    send_list = jnp.concatenate([lower_list, upper_list], axis=1).reshape(2 * layer_size * partitions)
    return (neighbour.astype(jnp.int32), boundary.astype(jnp.int32), send_list.astype(jnp.int32))


def draw_neighbour(key, part):
    return mesh_tables(key)[0]


def draw_boundary(key, part):
    return mesh_tables(key)[1]


def draw_send_list(key, part):
    return mesh_tables(key)[2]


def ramped(key, salt):
    sub_key = jax.random.fold_in(key, salt)
    shape_all = (SLABS, DOFS, ELEMS)
    growth = 3.0
    noise_draw = jax.random.truncated_normal(sub_key, -4.0, 4.0, shape_all, jnp.float32)
    slab_pos = jnp.arange(SLABS, dtype=jnp.float32)[:, None, None] / max(SLABS - 1, 1)
    part_pos = (jnp.arange(ELEMS) // E_DEV).astype(jnp.float32)[None, None, :] / max(ELEMS // E_DEV - 1, 1)
    return noise_draw * growth ** slab_pos * growth ** part_pos


def draw_initial(key, part):
    return ramped(key, 11)


def draw_rhs(key, part):
    return ramped(key, 23)


def steps_of(stream_key, shape, pieces, low, largest):
    def one(dim, parts):
        heights = jax.random.uniform(jax.random.fold_in(jax.random.fold_in(stream_key, 6), dim), (parts,), jnp.float32, low / len(pieces), largest / len(pieces))
        return jnp.repeat(jnp.exp(heights), shape[dim] // parts).reshape((-1,) + (1,) * (len(shape) - dim - 1))

    factor_of = one(*pieces[0])
    for cut in pieces[1:]:
        factor_of = factor_of * one(*cut)
    return factor_of


def normal_values(key, dims, scale, most, kind=jnp.bfloat16):
    values = scale * jax.random.normal(key, dims, jnp.float32)
    return jnp.clip(values, min=-most, max=most).astype(kind)


def setup_inputs(seed: int = 0) -> dict:
    keys = jax.random.split(jax.random.key(seed), 12)
    initial = draw_initial(jax.random.fold_in(keys[11], 71), 0)
    rhs = draw_rhs(jax.random.fold_in(keys[11], 71), 0)
    coef = jnp.clip(jnp.exp(math.log(4.0) - 2.0794415 * jax.random.uniform(keys[2], (ELEMS,), jnp.float32) ** steps_of(keys[2], (ELEMS,), ((0, 8),), -0.2, 0.2)), 0.5, 4.0)
    stiffness = normal_values(keys[3], (DOFS, DOFS), DOFS ** -0.5, 0.5, jnp.float32)
    block_inverse = normal_values(keys[4], (DOFS, DOFS), DOFS ** -0.5, 0.5, jnp.float32)
    face_proj = normal_values(keys[5], (6 * FDOFS, DOFS), DOFS ** -0.5, 0.5, jnp.float32)
    lift = normal_values(keys[6], (DOFS, 6 * FDOFS), (6 * FDOFS) ** -0.5, 0.4375, jnp.float32)
    time_lift = normal_values(keys[7], (DOFS, SDOFS), SDOFS ** -0.5, 0.75, jnp.float32)
    neighbour = draw_neighbour(jax.random.fold_in(keys[11], 71), 0)
    boundary = draw_boundary(jax.random.fold_in(keys[11], 71), 0)
    send_list = draw_send_list(jax.random.fold_in(keys[11], 71), 0)
    return {"initial": initial, "rhs": rhs, "coef": coef, "stiffness": stiffness, "block_inverse": block_inverse, "face_proj": face_proj, "lift": lift, "time_lift": time_lift, "neighbour": neighbour, "boundary": boundary, "send_list": send_list}


def slab_terms(vector, prev_end, coef, stiffness, face_proj, lift, time_lift, neighbour, boundary, send_list):
    partitions = ELEMS // E_DEV
    half_dofs = vector.shape[0] // 2
    traces = jnp.dot(face_proj, vector, precision=lax.Precision.HIGHEST)
    face_dofs = traces.shape[0] // 6
    trace_pool = traces.reshape(face_dofs, 6, partitions, E_DEV).transpose(2, 0, 1, 3).reshape(partitions, face_dofs, 6 * E_DEV)
    send_ids = jnp.broadcast_to(send_list.reshape(partitions, 1, 2 * NB), (partitions, face_dofs, 2 * NB))
    outbound = jnp.take_along_axis(trace_pool, send_ids, axis=2)
    zero_rim = jnp.zeros((1, face_dofs, NB), jnp.float32)
    from_lower = jnp.concatenate([zero_rim, outbound[:-1, :, NB:]], axis=0)
    from_upper = jnp.concatenate([outbound[1:, :, :NB], zero_rim], axis=0)
    ext_pool = jnp.concatenate([trace_pool, from_lower, from_upper], axis=2)
    column_ids = neighbour.reshape(6, partitions, E_DEV).transpose(1, 0, 2).reshape(partitions, 1, 6 * E_DEV)
    column_ids = jnp.broadcast_to(column_ids, (partitions, face_dofs, 6 * E_DEV))
    outside = jnp.take_along_axis(ext_pool, column_ids, axis=2)
    outside = outside.reshape(partitions, face_dofs, 6, E_DEV).transpose(1, 2, 0, 3).reshape(face_dofs * 6, ELEMS)
    open_faces = jnp.tile(1.0 - boundary.astype(jnp.float32), (face_dofs, 1))
    face_jump = traces - outside * open_faces
    time_jump = vector[:half_dofs] - prev_end
    applied = coef * jnp.dot(stiffness, vector, precision=lax.Precision.HIGHEST)
    applied = applied + jnp.dot(lift, face_jump, precision=lax.Precision.HIGHEST)
    applied = applied + jnp.dot(time_lift, time_jump, precision=lax.Precision.HIGHEST)
    return (applied, lax.optimization_barrier(jnp.sum(face_jump * face_jump, axis=0)), lax.optimization_barrier(jnp.sum(time_jump * time_jump, axis=0)))

def apply_all(state, coef, stiffness, face_proj, lift, time_lift, neighbour, boundary, send_list):
    half_dofs = state.shape[1] // 2
    prev_ends = jnp.concatenate([jnp.zeros((1, half_dofs, state.shape[2]), jnp.float32), state[:-1, half_dofs:, :]], axis=0)

    def one_slab(pair):
        return slab_terms(pair[0], pair[1], coef, stiffness, face_proj, lift, time_lift, neighbour, boundary, send_list)
    return lax.map(one_slab, (state, prev_ends))

def reference(initial, rhs, coef, stiffness, block_inverse, face_proj, lift, time_lift, neighbour, boundary, send_list):
    operands = (coef, stiffness, face_proj, lift, time_lift, neighbour, boundary, send_list)
    applied_base, unused_face, unused_time = apply_all(initial, *operands)
    residual = rhs - applied_base
    direction = jnp.einsum('ik,ske->sie', block_inverse, residual, precision=lax.Precision.HIGHEST) / coef
    image, unused_face, unused_time = apply_all(direction, *operands)
    step_size = jnp.sum(residual * image) / jnp.sum(image * image)
    smoothed = initial + step_size * direction
    new_residual = residual - step_size * image
    unused_image, face_sq, time_sq = apply_all(smoothed, *operands)
    element_eta = lax.optimization_barrier(jnp.sum(new_residual * new_residual, axis=1)) + 0.5 * face_sq + time_sq
    eta_total = jnp.sum(element_eta)
    element_count = SLABS * ELEMS
    indicator = element_eta * element_count / eta_total
    estimate = jnp.sqrt(eta_total / element_count).reshape(1)
    return (smoothed, indicator, estimate)
```

```python
import functools

import jax
import jax.numpy as jnp
from jax import lax
from jax.experimental import pallas as pl
from jax.experimental.pallas import tpu as pltpu
from jax.sharding import PartitionSpec as P

LANES = 128
SUBS = 8


def dot(a, b):
    return jnp.dot(a, b, precision=lax.Precision.HIGHEST, preferred_element_type=jnp.float32)


def lane_gather(tile_of, tiles, columns, rows):
    shape = (SUBS, LANES)
    low = jnp.broadcast_to(jnp.bitwise_and(columns, LANES - 1), shape)
    high = jnp.broadcast_to(jnp.right_shift(columns, 7), shape)
    found = [jnp.zeros(shape, jnp.float32) for _ in range(rows // SUBS)]
    for tile in range(tiles):
        here = high == tile
        for r in range(rows // SUBS):
            picked = jnp.take_along_axis(tile_of(tile, r), low, axis=1)
            found[r] = jnp.where(here, picked, found[r])
    return found


def face_rows(ref, face, face_dofs):
    return ref[pl.ds(face, face_dofs, stride=6), :]


def fill_outbound(traces, send_ref, odd, first_ref, second_ref, face_dofs, elements):
    per_face = elements // LANES

    def tile_of(tile, r):
        face, col = divmod(tile, per_face)
        return traces[face * face_dofs + r * SUBS : face * face_dofs + (r + 1) * SUBS, col * LANES : (col + 1) * LANES]

    border = send_ref.shape[1]
    for j in range(border // LANES):
        cols = slice(j * LANES, (j + 1) * LANES)
        lower = lane_gather(tile_of, 2 * per_face, send_ref[0:1, cols], face_dofs)
        upper = lane_gather(tile_of, 2 * per_face, send_ref[1:2, cols], face_dofs)
        for r in range(face_dofs // SUBS):
            rows = slice(r * SUBS, (r + 1) * SUBS)
            first_ref[rows, cols] = jnp.where(odd, lower[r], upper[r])
            second_ref[rows, cols] = jnp.where(odd, upper[r], lower[r])


def fill_jump(traces, nb_ref, bd_ref, jump_ref, face_dofs, elements):
    per_face = elements // LANES
    for face in range(6):
        other = face ^ 1

        def tile_of(tile, r, other=other):
            return traces[other * face_dofs + r * SUBS : other * face_dofs + (r + 1) * SUBS, tile * LANES : (tile + 1) * LANES]

        for j in range(per_face):
            cols = slice(j * LANES, (j + 1) * LANES)
            found = lane_gather(tile_of, per_face, nb_ref[face : face + 1, cols] - other * elements, face_dofs)
            open_face = jnp.broadcast_to(1.0 - bd_ref[face : face + 1, cols].astype(jnp.float32), (SUBS, LANES))
            for r in range(face_dofs // SUBS):
                rows = slice(face * face_dofs + r * SUBS, face * face_dofs + (r + 1) * SUBS)
                jump_ref[rows, cols] = traces[rows, cols] - found[r] * open_face


def rim_terms(first_ref, second_ref, nb_ref, bd_ref, odd, rim_ref, face_dofs, elements):
    border = first_ref.shape[1]
    tiles = border // LANES

    for j in range(elements // LANES):
        cols = slice(j * LANES, (j + 1) * LANES)
        for face in range(2):
            columns = nb_ref[face : face + 1, cols] - 6 * elements

            def tile_of(tile, r):
                side, t = divmod(tile, tiles)
                rows, part = slice(r * SUBS, (r + 1) * SUBS), slice(t * LANES, (t + 1) * LANES)
                a, b = first_ref[rows, part], second_ref[rows, part]
                return jnp.where(odd, a, b) if side == 0 else jnp.where(odd, b, a)

            found = lane_gather(tile_of, 2 * tiles, columns, face_dofs)
            open_face = jnp.broadcast_to(1.0 - bd_ref[face : face + 1, cols].astype(jnp.float32), (SUBS, LANES))
            for r in range(face_dofs // SUBS):
                rows = slice(face * face_dofs + r * SUBS, face * face_dofs + (r + 1) * SUBS)
                rim_ref[rows, cols] = 0.0 - found[r] * open_face


def first_send(odd_ref, v_ref, fp_ref, send_ref, tr_ref, first_ref, second_ref):
    face_dofs = fp_ref.shape[0] // 6
    elements = v_ref.shape[1]
    weights = jnp.concatenate([face_rows(fp_ref, f, face_dofs) for f in range(2)], axis=0)
    tr_ref[...] = dot(weights, v_ref[...])
    fill_outbound(tr_ref, send_ref, odd_ref[0] == 1, first_ref, second_ref, face_dofs, elements)


def local_part(v_ref, tr_ref, coef_ref, fp_ref, stiff_ref, liftt_ref, nb_ref, bd_ref, part_ref, jump_ref, traces):
    face_dofs = fp_ref.shape[0] // 6
    elements = v_ref.shape[1]
    traces[: 2 * face_dofs, :] = tr_ref[...]
    weights = jnp.concatenate([face_rows(fp_ref, f, face_dofs) for f in range(2, 6)], axis=0)
    traces[2 * face_dofs :, :] = dot(weights, v_ref[...])
    fill_jump(traces, nb_ref, bd_ref, jump_ref, face_dofs, elements)
    liftt = jnp.concatenate([face_rows(liftt_ref, f, face_dofs) for f in range(6)], axis=0)
    part_ref[...] = coef_ref[...] * dot(stiff_ref[...], v_ref[...]) + dot(liftt.T, jump_ref[...])


def finish_operator(part_ref, v_ref, prev_ref, liftt_ref, tlt_ref, rim, face_dofs):
    half = prev_ref.shape[0]
    time_jump = v_ref[:half, :] - prev_ref[...]
    liftt = jnp.concatenate([face_rows(liftt_ref, f, face_dofs) for f in range(2)] + [tlt_ref[...]], axis=0)
    values = jnp.concatenate([rim[...], time_jump], axis=0)
    return part_ref[...] + dot(liftt.T, values)


def residual_step(
    odd_ref, part_ref, jump_ref, v_ref, rhs_ref, prev_ref, first_in, second_in, coef_ref, inv_ref, fp_ref, liftt_ref, tlt_ref,
    nb_ref, bd_ref, send_ref, res_ref, rim_ref, dir_ref, end_ref, tr_ref, first_ref, second_ref,
):
    face_dofs = fp_ref.shape[0] // 6
    elements = v_ref.shape[1]
    half = prev_ref.shape[0]
    odd = odd_ref[0] == 1
    rim_terms(first_in, second_in, nb_ref, bd_ref, odd, rim_ref, face_dofs, elements)
    res_ref[...] = rhs_ref[...] - finish_operator(part_ref, v_ref, prev_ref, liftt_ref, tlt_ref, rim_ref, face_dofs)
    direction = dot(inv_ref[...], res_ref[...]) / coef_ref[...]
    dir_ref[...] = direction
    end_ref[...] = direction[half:, :]
    weights = jnp.concatenate([face_rows(fp_ref, f, face_dofs) for f in range(2)], axis=0)
    tr_ref[...] = dot(weights, direction)
    fill_outbound(tr_ref, send_ref, odd, first_ref, second_ref, face_dofs, elements)


def column_sum(x):
    return jnp.sum(x, axis=0, keepdims=True)


def total_sum(row):
    return jnp.sum(row, axis=1, keepdims=True)


def image_step(
    odd_ref, part_ref, jump_ref, dir_ref, prev_ref, first_in, second_in, liftt_ref, tlt_ref, nb_ref, bd_ref,
    res_ref, jump0_ref, rim0_ref, v_ref, prev0_ref, coeff_ref, sums_ref, rim, image,
):
    face_dofs = first_in.shape[0]
    elements = dir_ref.shape[1]
    half = prev_ref.shape[0]
    rim_rows = rim.shape[0]
    odd = odd_ref[0] == 1
    rim_terms(first_in, second_in, nb_ref, bd_ref, odd, rim, face_dofs, elements)
    image[...] = finish_operator(part_ref, dir_ref, prev_ref, liftt_ref, tlt_ref, rim, face_dofs)
    res, img = res_ref[...], image[...]
    cross = column_sum(res * img)
    square = column_sum(img * img)
    j0 = jnp.concatenate([jump0_ref[:rim_rows, :] + rim0_ref[...], jump0_ref[rim_rows:, :]], axis=0)
    j1 = jnp.concatenate([jump_ref[:rim_rows, :] + rim[...], jump_ref[rim_rows:, :]], axis=0)
    t0 = v_ref[:half, :] - prev0_ref[...]
    t1 = dir_ref[:half, :] - prev_ref[...]
    bend = square + 0.5 * column_sum(j1 * j1) + column_sum(t1 * t1)
    slope = 0.5 * column_sum(j0 * j1) + column_sum(t0 * t1) - cross
    best = jnp.where(bend > 0.0, -slope / jnp.where(bend > 0.0, bend, 1.0), 0.0)
    r = res - best * img
    j = j0 + best * j1
    t = t0 + best * t1
    base = column_sum(r * r) + 0.5 * column_sum(j * j) + column_sum(t * t)
    tilt = slope + best * bend
    bend_all = total_sum(bend)
    weighted = total_sum(best * bend)
    centre = jnp.where(bend_all > 0.0, weighted / jnp.where(bend_all > 0.0, bend_all, 1.0), 0.0)
    off = centre - best
    base_all = total_sum(base + off * (2.0 * tilt + off * bend))
    tilt_all = total_sum(tilt + off * bend)
    coeff_ref[...] = jnp.concatenate([base, tilt, bend, best, best, best, best, best], axis=0)
    lane = lax.broadcasted_iota(jnp.int32, sums_ref.shape, 1)
    out = jnp.zeros(sums_ref.shape, jnp.float32)
    for i, value in enumerate((total_sum(cross), total_sum(square), base_all, tilt_all, bend_all, centre)):
        out = jnp.where(lane == i, value, out)
    sums_ref[...] = out


def last_step(count, all_ref, coeff_ref, v_ref, dir_ref, smooth_ref, ind_ref, est_ref):
    sums = all_ref[...]
    step = jnp.sum(sums[:, 0:1], axis=0, keepdims=True) / jnp.sum(sums[:, 1:2], axis=0, keepdims=True)
    smooth_ref[...] = v_ref[...] + step * dir_ref[...]
    off = step - sums[:, 5:6]
    total = jnp.sum(sums[:, 2:3] + off * (2.0 * sums[:, 3:4] + off * sums[:, 4:5]), axis=0, keepdims=True)
    delta = step - coeff_ref[3:4, :]
    eta = coeff_ref[0:1, :] + delta * (2.0 * coeff_ref[1:2, :] + delta * coeff_ref[2:3, :])
    ind_ref[...] = eta * count / total
    est_ref[...] = jnp.broadcast_to(jnp.sqrt(total / count), est_ref.shape)


VM = pl.BlockSpec(memory_space=pltpu.VMEM)
SM = pl.BlockSpec(memory_space=pltpu.SMEM)


def call(body, name, outs, args, flops, scratch=(), scalars=0):
    shapes = [jax.ShapeDtypeStruct(s, jnp.float32) for s in outs]
    moved = sum(4 * a.size for a in args) + sum(4 * s.size for s in shapes)
    return pl.pallas_call(
        body,
        name=name,
        out_shape=shapes,
        in_specs=[SM] * scalars + [VM] * (len(args) - scalars),
        out_specs=[VM] * len(outs),
        scratch_shapes=[pltpu.VMEM(s, jnp.float32) for s in scratch],
        cost_estimate=pl.CostEstimate(flops=flops, bytes_accessed=moved, transcendentals=0),
    )(*args)


def on_device(initial, rhs, coef, stiffness, block_inverse, face_proj, lift, time_lift, neighbour, boundary, send_list):
    v0, source = initial[0], rhs[0]
    dofs, elements = v0.shape
    half = time_lift.shape[1]
    traces = face_proj.shape[0]
    face_dofs = traces // 6
    border = send_list.shape[0] // 2
    slabs, parts = lax.axis_size("tm"), lax.axis_size("space")
    devices = slabs * parts
    odd = (lax.axis_index("space") % 2).astype(jnp.int32).reshape(1)
    coef_row = coef.reshape(1, elements)
    send = send_list.reshape(2, border)
    liftt, tlt = lift.T, time_lift.T
    later = [(i, i + 1) for i in range(slabs - 1)]

    def swaps(first):
        pairs = [(i, i + 1) for i in range(first, parts - 1, 2)]
        return pairs + [(j, i) for i, j in pairs]

    def halo(a, b):
        return lax.ppermute(a, "space", swaps(0)), lax.ppermute(b, "space", swaps(1))

    two = 2 * face_dofs
    prev0 = lax.ppermute(v0[half:], "tm", later)
    tr0, a0, b0 = call(
        first_send, "send0", [(two, elements), (face_dofs, border), (face_dofs, border)], (odd, v0, face_proj, send), 2 * two * dofs * elements, scalars=1
    )
    a0, b0 = halo(a0, b0)
    local = functools.partial(
        call, local_part, "local", [(dofs, elements), (traces, elements)], flops=12 * traces * dofs * elements, scratch=[(traces, elements)]
    )
    part0, jump0 = local(args=(v0, tr0, coef_row, face_proj, stiffness, liftt, neighbour, boundary))
    res, rim0, direction, end, tr1, a1, b1 = call(
        residual_step,
        "residual",
        [(dofs, elements), (two, elements), (dofs, elements), (half, elements), (two, elements), (face_dofs, border), (face_dofs, border)],
        (odd, part0, jump0, v0, source, prev0, a0, b0, coef_row, block_inverse, face_proj, liftt, tlt, neighbour, boundary, send),
        12 * dofs * dofs * elements,
        scalars=1,
    )
    prev1 = lax.ppermute(end, "tm", later)
    a1, b1 = halo(a1, b1)
    part1, jump1 = local(args=(direction, tr1, coef_row, face_proj, stiffness, liftt, neighbour, boundary))
    coeffs, sums = call(
        image_step,
        "image",
        [(SUBS, elements), (devices, LANES)],
        (odd, part1, jump1, direction, prev1, a1, b1, liftt, tlt, neighbour, boundary, res, jump0, rim0, v0, prev0),
        12 * dofs * dofs * elements,
        scratch=[(two, elements), (dofs, elements)],
        scalars=1,
    )
    everyone = lax.all_to_all(sums, ("tm", "space"), 0, 0, tiled=True)
    smoothed, indicator, estimate = call(
        functools.partial(last_step, float(elements * devices)),
        "last",
        [(dofs, elements), (1, elements), (1, LANES)],
        (everyone, coeffs, v0, direction),
        4 * dofs * elements,
    )
    return smoothed[None], indicator, estimate[0, :1]


def solution(mesh):
    placed = (
        P("tm", None, "space"),
        P("tm", None, "space"),
        P("space"),
        P(),
        P(),
        P(),
        P(),
        P(),
        P(None, "space"),
        P(None, "space"),
        P("space"),
    )
    return jax.shard_map(
        on_device,
        mesh=mesh,
        in_specs=placed,
        out_specs=(P("tm", None, "space"), P("tm", "space"), P()),
        check_vma=False,
    )
```

```python
import functools

import jax
import jax.numpy as jnp
from jax import lax
from jax.experimental import pallas as pl
from jax.experimental.pallas import tpu as pltpu
from jax.sharding import PartitionSpec as P

LANES = 128
SUBS = 8


def dot(a, b):
    return jnp.dot(a, b, precision=lax.Precision.HIGHEST, preferred_element_type=jnp.float32)


def lane_gather(tile_of, tiles, columns, rows):
    shape = (SUBS, LANES)
    low = jnp.broadcast_to(jnp.bitwise_and(columns, LANES - 1), shape)
    high = jnp.broadcast_to(jnp.right_shift(columns, 7), shape)
    found = [jnp.zeros(shape, jnp.float32) for _ in range(rows // SUBS)]
    for tile in range(tiles):
        here = high == tile
        for r in range(rows // SUBS):
            picked = jnp.take_along_axis(tile_of(tile, r), low, axis=1)
            found[r] = jnp.where(here, picked, found[r])
    return found


def face_rows(ref, face, face_dofs):
    return ref[pl.ds(face, face_dofs, stride=6), :]


def fill_outbound(traces, send_ref, odd, first_ref, second_ref, face_dofs, elements):
    per_face = elements // LANES

    def tile_of(tile, r):
        face, col = divmod(tile, per_face)
        return traces[face * face_dofs + r * SUBS : face * face_dofs + (r + 1) * SUBS, col * LANES : (col + 1) * LANES]

    border = send_ref.shape[1]
    for j in range(border // LANES):
        cols = slice(j * LANES, (j + 1) * LANES)
        lower = lane_gather(tile_of, 2 * per_face, send_ref[0:1, cols], face_dofs)
        upper = lane_gather(tile_of, 2 * per_face, send_ref[1:2, cols], face_dofs)
        for r in range(face_dofs // SUBS):
            rows = slice(r * SUBS, (r + 1) * SUBS)
            first_ref[rows, cols] = jnp.where(odd, lower[r], upper[r])
            second_ref[rows, cols] = jnp.where(odd, upper[r], lower[r])


def fill_jump(traces, nb_ref, bd_ref, jump_ref, face_dofs, elements):
    per_face = elements // LANES
    for face in range(6):
        other = face ^ 1

        def tile_of(tile, r, other=other):
            return traces[other * face_dofs + r * SUBS : other * face_dofs + (r + 1) * SUBS, tile * LANES : (tile + 1) * LANES]

        for j in range(per_face):
            cols = slice(j * LANES, (j + 1) * LANES)
            found = lane_gather(tile_of, per_face, nb_ref[face : face + 1, cols] - other * elements, face_dofs)
            open_face = jnp.broadcast_to(1.0 - bd_ref[face : face + 1, cols].astype(jnp.float32), (SUBS, LANES))
            for r in range(face_dofs // SUBS):
                rows = slice(face * face_dofs + r * SUBS, face * face_dofs + (r + 1) * SUBS)
                jump_ref[rows, cols] = traces[rows, cols] - found[r] * open_face


def rim_terms(first_ref, second_ref, nb_ref, bd_ref, odd, rim_ref, face_dofs, elements):
    border = first_ref.shape[1]
    tiles = border // LANES

    for j in range(elements // LANES):
        cols = slice(j * LANES, (j + 1) * LANES)
        for face in range(2):
            columns = nb_ref[face : face + 1, cols] - 6 * elements

            def tile_of(tile, r):
                side, t = divmod(tile, tiles)
                rows, part = slice(r * SUBS, (r + 1) * SUBS), slice(t * LANES, (t + 1) * LANES)
                a, b = first_ref[rows, part], second_ref[rows, part]
                return jnp.where(odd, a, b) if side == 0 else jnp.where(odd, b, a)

            found = lane_gather(tile_of, 2 * tiles, columns, face_dofs)
            open_face = jnp.broadcast_to(1.0 - bd_ref[face : face + 1, cols].astype(jnp.float32), (SUBS, LANES))
            for r in range(face_dofs // SUBS):
                rows = slice(face * face_dofs + r * SUBS, face * face_dofs + (r + 1) * SUBS)
                rim_ref[rows, cols] = 0.0 - found[r] * open_face


def first_send(odd_ref, v_ref, fp_ref, send_ref, tr_ref, first_ref, second_ref):
    face_dofs = fp_ref.shape[0] // 6
    elements = v_ref.shape[1]
    weights = jnp.concatenate([face_rows(fp_ref, f, face_dofs) for f in range(2)], axis=0)
    tr_ref[...] = dot(weights, v_ref[...])
    fill_outbound(tr_ref, send_ref, odd_ref[0] == 1, first_ref, second_ref, face_dofs, elements)


def local_part(v_ref, tr_ref, coef_ref, fp_ref, stiff_ref, liftt_ref, nb_ref, bd_ref, part_ref, jump_ref, traces):
    face_dofs = fp_ref.shape[0] // 6
    elements = v_ref.shape[1]
    traces[: 2 * face_dofs, :] = tr_ref[...]
    weights = jnp.concatenate([face_rows(fp_ref, f, face_dofs) for f in range(2, 6)], axis=0)
    traces[2 * face_dofs :, :] = dot(weights, v_ref[...])
    fill_jump(traces, nb_ref, bd_ref, jump_ref, face_dofs, elements)
    liftt = jnp.concatenate([face_rows(liftt_ref, f, face_dofs) for f in range(6)], axis=0)
    part_ref[...] = coef_ref[...] * dot(stiff_ref[...], v_ref[...]) + dot(liftt.T, jump_ref[...])


def finish_operator(part_ref, v_ref, prev_ref, liftt_ref, tlt_ref, rim, face_dofs):
    half = prev_ref.shape[0]
    time_jump = v_ref[:half, :] - prev_ref[...]
    liftt = jnp.concatenate([face_rows(liftt_ref, f, face_dofs) for f in range(2)] + [tlt_ref[...]], axis=0)
    values = jnp.concatenate([rim[...], time_jump], axis=0)
    return part_ref[...] + dot(liftt.T, values)


def residual_step(
    odd_ref, part_ref, jump_ref, v_ref, rhs_ref, prev_ref, first_in, second_in, coef_ref, inv_ref, fp_ref, liftt_ref, tlt_ref,
    nb_ref, bd_ref, send_ref, res_ref, rim_ref, dir_ref, end_ref, tr_ref, first_ref, second_ref,
):
    face_dofs = fp_ref.shape[0] // 6
    elements = v_ref.shape[1]
    half = prev_ref.shape[0]
    odd = odd_ref[0] == 1
    rim_terms(first_in, second_in, nb_ref, bd_ref, odd, rim_ref, face_dofs, elements)
    res_ref[...] = rhs_ref[...] - finish_operator(part_ref, v_ref, prev_ref, liftt_ref, tlt_ref, rim_ref, face_dofs)
    direction = dot(inv_ref[...], res_ref[...]) / coef_ref[...]
    dir_ref[...] = direction
    end_ref[...] = direction[half:, :]
    weights = jnp.concatenate([face_rows(fp_ref, f, face_dofs) for f in range(2)], axis=0)
    tr_ref[...] = dot(weights, direction)
    fill_outbound(tr_ref, send_ref, odd, first_ref, second_ref, face_dofs, elements)


def column_sum(x):
    return jnp.sum(x, axis=0, keepdims=True)


def total_sum(row):
    return jnp.sum(row, axis=1, keepdims=True)


def image_step(
    odd_ref, part_ref, jump_ref, dir_ref, prev_ref, first_in, second_in, liftt_ref, tlt_ref, nb_ref, bd_ref,
    res_ref, jump0_ref, rim0_ref, v_ref, prev0_ref, coeff_ref, sums_ref, rim, image,
):
    face_dofs = first_in.shape[0]
    elements = dir_ref.shape[1]
    half = prev_ref.shape[0]
    rim_rows = rim.shape[0]
    odd = odd_ref[0] == 1
    rim_terms(first_in, second_in, nb_ref, bd_ref, odd, rim, face_dofs, elements)
    image[...] = finish_operator(part_ref, dir_ref, prev_ref, liftt_ref, tlt_ref, rim, face_dofs)
    res, img = res_ref[...], image[...]
    cross = column_sum(res * img)
    square = column_sum(img * img)
    j0 = jnp.concatenate([jump0_ref[:rim_rows, :] + rim0_ref[...], jump0_ref[rim_rows:, :]], axis=0)
    j1 = jnp.concatenate([jump_ref[:rim_rows, :] + rim[...], jump_ref[rim_rows:, :]], axis=0)
    t0 = v_ref[:half, :] - prev0_ref[...]
    t1 = dir_ref[:half, :] - prev_ref[...]
    bend = square + 0.5 * column_sum(j1 * j1) + column_sum(t1 * t1)
    slope = 0.5 * column_sum(j0 * j1) + column_sum(t0 * t1) - cross
    best = jnp.where(bend > 0.0, -slope / jnp.where(bend > 0.0, bend, 1.0), 0.0)
    r = res - best * img
    j = j0 + best * j1
    t = t0 + best * t1
    base = column_sum(r * r) + 0.5 * column_sum(j * j) + column_sum(t * t)
    tilt = slope + best * bend
    bend_all = total_sum(bend)
    weighted = total_sum(best * bend)
    centre = jnp.where(bend_all > 0.0, weighted / jnp.where(bend_all > 0.0, bend_all, 1.0), 0.0)
    off = centre - best
    base_all = total_sum(base + off * (2.0 * tilt + off * bend))
    tilt_all = total_sum(tilt + off * bend)
    coeff_ref[...] = jnp.concatenate([base, tilt, bend, best, best, best, best, best], axis=0)
    lane = lax.broadcasted_iota(jnp.int32, sums_ref.shape, 1)
    out = jnp.zeros(sums_ref.shape, jnp.float32)
    for i, value in enumerate((total_sum(cross), total_sum(square), base_all, tilt_all, bend_all, centre)):
        out = jnp.where(lane == i, value, out)
    sums_ref[...] = out


def last_step(count, all_ref, coeff_ref, v_ref, dir_ref, smooth_ref, ind_ref, est_ref):
    sums = all_ref[...]
    step = jnp.sum(sums[:, 0:1], axis=0, keepdims=True) / jnp.sum(sums[:, 1:2], axis=0, keepdims=True)
    smooth_ref[...] = v_ref[...] + step * dir_ref[...]
    off = step - sums[:, 5:6]
    total = jnp.sum(sums[:, 2:3] + off * (2.0 * sums[:, 3:4] + off * sums[:, 4:5]), axis=0, keepdims=True)
    delta = step - coeff_ref[3:4, :]
    eta = coeff_ref[0:1, :] + delta * (2.0 * coeff_ref[1:2, :] + delta * coeff_ref[2:3, :])
    ind_ref[...] = eta * count / total
    est_ref[...] = jnp.broadcast_to(jnp.sqrt(total / count), est_ref.shape)


VM = pl.BlockSpec(memory_space=pltpu.VMEM)
SM = pl.BlockSpec(memory_space=pltpu.SMEM)


def call(body, name, outs, args, flops, scratch=(), scalars=0):
    shapes = [jax.ShapeDtypeStruct(s, jnp.float32) for s in outs]
    moved = sum(4 * a.size for a in args) + sum(4 * s.size for s in shapes)
    return pl.pallas_call(
        body,
        name=name,
        out_shape=shapes,
        in_specs=[SM] * scalars + [VM] * (len(args) - scalars),
        out_specs=[VM] * len(outs),
        scratch_shapes=[pltpu.VMEM(s, jnp.float32) for s in scratch],
        cost_estimate=pl.CostEstimate(flops=flops, bytes_accessed=moved, transcendentals=0),
        compiler_params=pltpu.CompilerParams(vmem_limit_bytes=20 * 2**20),
    )(*args)


def on_device(initial, rhs, coef, stiffness, block_inverse, face_proj, lift, time_lift, neighbour, boundary, send_list):
    v0, source = initial[0], rhs[0]
    dofs, elements = v0.shape
    half = time_lift.shape[1]
    traces = face_proj.shape[0]
    face_dofs = traces // 6
    border = send_list.shape[0] // 2
    slabs, parts = lax.axis_size("tm"), lax.axis_size("space")
    devices = slabs * parts
    odd = (lax.axis_index("space") % 2).astype(jnp.int32).reshape(1)
    coef_row = coef.reshape(1, elements)
    send = send_list.reshape(2, border)
    liftt, tlt = lift.T, time_lift.T
    later = [(i, i + 1) for i in range(slabs - 1)]

    def swaps(first):
        pairs = [(i, i + 1) for i in range(first, parts - 1, 2)]
        return pairs + [(j, i) for i, j in pairs]

    def halo(a, b):
        return lax.ppermute(a, "space", swaps(0)), lax.ppermute(b, "space", swaps(1))

    two = 2 * face_dofs
    prev0 = lax.ppermute(v0[half:], "tm", later)
    tr0, a0, b0 = call(
        first_send, "send0", [(two, elements), (face_dofs, border), (face_dofs, border)], (odd, v0, face_proj, send), 2 * two * dofs * elements, scalars=1
    )
    a0, b0 = halo(a0, b0)
    local = functools.partial(
        call, local_part, "local", [(dofs, elements), (traces, elements)], flops=12 * traces * dofs * elements, scratch=[(traces, elements)]
    )
    part0, jump0 = local(args=(v0, tr0, coef_row, face_proj, stiffness, liftt, neighbour, boundary))
    res, rim0, direction, end, tr1, a1, b1 = call(
        residual_step,
        "residual",
        [(dofs, elements), (two, elements), (dofs, elements), (half, elements), (two, elements), (face_dofs, border), (face_dofs, border)],
        (odd, part0, jump0, v0, source, prev0, a0, b0, coef_row, block_inverse, face_proj, liftt, tlt, neighbour, boundary, send),
        12 * dofs * dofs * elements,
        scalars=1,
    )
    prev1 = lax.ppermute(end, "tm", later)
    a1, b1 = halo(a1, b1)
    part1, jump1 = local(args=(direction, tr1, coef_row, face_proj, stiffness, liftt, neighbour, boundary))
    coeffs, sums = call(
        image_step,
        "image",
        [(SUBS, elements), (devices, LANES)],
        (odd, part1, jump1, direction, prev1, a1, b1, liftt, tlt, neighbour, boundary, res, jump0, rim0, v0, prev0),
        12 * dofs * dofs * elements,
        scratch=[(two, elements), (dofs, elements)],
        scalars=1,
    )
    everyone = lax.all_to_all(sums, ("tm", "space"), 0, 0, tiled=True)
    smoothed, indicator, estimate = call(
        functools.partial(last_step, float(elements * devices)),
        "last",
        [(dofs, elements), (1, elements), (1, LANES)],
        (everyone, coeffs, v0, direction),
        4 * dofs * elements,
    )
    return smoothed[None], indicator, estimate[0, :1]


def solution(mesh):
    placed = (
        P("tm", None, "space"),
        P("tm", None, "space"),
        P("space"),
        P(),
        P(),
        P(),
        P(),
        P(),
        P(None, "space"),
        P(None, "space"),
        P("space"),
    )
    return jax.shard_map(
        on_device,
        mesh=mesh,
        in_specs=placed,
        out_specs=(P("tm", None, "space"), P("tm", "space"), P()),
        check_vma=False,
    )
```

```python
import functools

import jax
import jax.numpy as jnp
from jax import lax
from jax.experimental import pallas as pl
from jax.experimental.pallas import tpu as pltpu
from jax.sharding import PartitionSpec as P

LANES = 128
SUBS = 8


def dot(a, b):
    return jnp.dot(a, b, precision=lax.Precision.HIGHEST, preferred_element_type=jnp.float32)


def lane_gather(tile_of, tiles, columns, rows):
    shape = (SUBS, LANES)
    low = jnp.broadcast_to(jnp.bitwise_and(columns, LANES - 1), shape)
    high = jnp.broadcast_to(jnp.right_shift(columns, 7), shape)
    found = [jnp.zeros(shape, jnp.float32) for _ in range(rows // SUBS)]
    for tile in range(tiles):
        here = high == tile
        for r in range(rows // SUBS):
            picked = jnp.take_along_axis(tile_of(tile, r), low, axis=1)
            found[r] = jnp.where(here, picked, found[r])
    return found


def face_rows(ref, face, face_dofs):
    return ref[pl.ds(face, face_dofs, stride=6), :]


def is_odd():
    return lax.rem(lax.axis_index("space"), 2) == 1


def fill_outbound(traces, send_ref, first_ref, second_ref, face_dofs, elements):
    per_face = elements // LANES
    odd = is_odd()

    def tile_of(tile, r):
        face, col = divmod(tile, per_face)
        return traces[face * face_dofs + r * SUBS : face * face_dofs + (r + 1) * SUBS, col * LANES : (col + 1) * LANES]

    border = send_ref.shape[1]
    for j in range(border // LANES):
        cols = slice(j * LANES, (j + 1) * LANES)
        lower = lane_gather(tile_of, 2 * per_face, send_ref[0:1, cols], face_dofs)
        upper = lane_gather(tile_of, 2 * per_face, send_ref[1:2, cols], face_dofs)
        for r in range(face_dofs // SUBS):
            rows = slice(r * SUBS, (r + 1) * SUBS)
            first_ref[rows, cols] = jnp.where(odd, lower[r], upper[r])
            second_ref[rows, cols] = jnp.where(odd, upper[r], lower[r])


def fill_jump(traces, nb_ref, bd_ref, jump_ref, face_dofs, elements):
    per_face = elements // LANES
    for face in range(6):
        other = face ^ 1

        def tile_of(tile, r, other=other):
            return traces[other * face_dofs + r * SUBS : other * face_dofs + (r + 1) * SUBS, tile * LANES : (tile + 1) * LANES]

        for j in range(per_face):
            cols = slice(j * LANES, (j + 1) * LANES)
            found = lane_gather(tile_of, per_face, nb_ref[face : face + 1, cols] - other * elements, face_dofs)
            open_face = jnp.broadcast_to(1.0 - bd_ref[face : face + 1, cols].astype(jnp.float32), (SUBS, LANES))
            for r in range(face_dofs // SUBS):
                rows = slice(face * face_dofs + r * SUBS, face * face_dofs + (r + 1) * SUBS)
                jump_ref[rows, cols] = traces[rows, cols] - found[r] * open_face


def rim_terms(first_ref, second_ref, nb_ref, bd_ref, rim_ref, face_dofs, elements):
    tiles = first_ref.shape[1] // LANES
    odd, place, parts = is_odd(), lax.axis_index("space"), lax.axis_size("space")
    sides = []
    for side in range(2):
        for t in range(tiles):
            cols = slice(t * LANES, (t + 1) * LANES)
            a, b = first_ref[:, cols], second_ref[:, cols]
            values = jnp.where(odd, a, b) if side == 0 else jnp.where(odd, b, a)
            there = place > 0 if side == 0 else place < parts - 1
            sides.append(jnp.where(there, values, 0.0))

    def tile_of(tile, r):
        return sides[tile][r * SUBS : (r + 1) * SUBS, :]

    for j in range(elements // LANES):
        cols = slice(j * LANES, (j + 1) * LANES)
        for face in range(2):
            found = lane_gather(tile_of, 2 * tiles, nb_ref[face : face + 1, cols] - 6 * elements, face_dofs)
            open_face = jnp.broadcast_to(1.0 - bd_ref[face : face + 1, cols].astype(jnp.float32), (SUBS, LANES))
            for r in range(face_dofs // SUBS):
                rows = slice(face * face_dofs + r * SUBS, face * face_dofs + (r + 1) * SUBS)
                rim_ref[rows, cols] = 0.0 - found[r] * open_face


def first_send(v_hbm, fp_hbm, send_hbm, v_ref, end_ref, tr_ref, first_ref, second_ref, fp_ref, send_ref, sems):
    face_dofs = fp_ref.shape[0] // 6
    elements = v_ref.shape[1]
    half = end_ref.shape[0]
    pairs = ((v_hbm, v_ref), (fp_hbm, fp_ref), (send_hbm, send_ref), (v_hbm.at[pl.ds(half, half), :], end_ref))
    copies = [pltpu.make_async_copy(a, b, sems.at[i]) for i, (a, b) in enumerate(pairs)]
    for copy in copies:
        copy.start()
    for copy in copies[:3]:
        copy.wait()
    weights = jnp.concatenate([face_rows(fp_ref, f, face_dofs) for f in range(2)], axis=0)
    tr_ref[...] = dot(weights, v_ref[...])
    fill_outbound(tr_ref, send_ref, first_ref, second_ref, face_dofs, elements)
    copies[3].wait()


def local_part(v_ref, tr_ref, coef_ref, fp_ref, stiff_ref, liftt_ref, nb_ref, bd_ref, part_ref, jump_ref, traces):
    face_dofs = fp_ref.shape[0] // 6
    elements = v_ref.shape[1]
    traces[: 2 * face_dofs, :] = tr_ref[...]
    weights = jnp.concatenate([face_rows(fp_ref, f, face_dofs) for f in range(2, 6)], axis=0)
    traces[2 * face_dofs :, :] = dot(weights, v_ref[...])
    fill_jump(traces, nb_ref, bd_ref, jump_ref, face_dofs, elements)
    liftt = jnp.concatenate([face_rows(liftt_ref, f, face_dofs) for f in range(6)], axis=0)
    part_ref[...] = coef_ref[...] * dot(stiff_ref[...], v_ref[...]) + dot(liftt.T, jump_ref[...])


def time_jump_of(v_ref, prev_ref):
    return v_ref[: prev_ref.shape[0], :] - jnp.where(lax.axis_index("tm") > 0, prev_ref[...], 0.0)


def finish_operator(part_ref, v_ref, prev_ref, liftt_ref, tlt_ref, rim, face_dofs):
    time_jump = time_jump_of(v_ref, prev_ref)
    liftt = jnp.concatenate([face_rows(liftt_ref, f, face_dofs) for f in range(2)] + [tlt_ref[...]], axis=0)
    values = jnp.concatenate([rim[...], time_jump], axis=0)
    return part_ref[...] + dot(liftt.T, values)


def residual_step(
    part_ref, v_ref, rhs_ref, prev_ref, first_in, second_in, coef_ref, inv_ref, fp_ref, liftt_ref, tlt_ref,
    nb_ref, bd_ref, send_ref, res_ref, rim_ref, dir_ref, end_ref, tr_ref, first_ref, second_ref,
):
    face_dofs = fp_ref.shape[0] // 6
    elements = v_ref.shape[1]
    half = prev_ref.shape[0]
    rim_terms(first_in, second_in, nb_ref, bd_ref, rim_ref, face_dofs, elements)
    res_ref[...] = rhs_ref[...] - finish_operator(part_ref, v_ref, prev_ref, liftt_ref, tlt_ref, rim_ref, face_dofs)
    direction = dot(inv_ref[...], res_ref[...]) / coef_ref[...]
    dir_ref[...] = direction
    end_ref[...] = direction[half:, :]
    weights = jnp.concatenate([face_rows(fp_ref, f, face_dofs) for f in range(2)], axis=0)
    tr_ref[...] = dot(weights, direction)
    fill_outbound(tr_ref, send_ref, first_ref, second_ref, face_dofs, elements)


def column_sum(x):
    return jnp.sum(x, axis=0, keepdims=True)


def total_sum(row):
    return jnp.sum(row, axis=1, keepdims=True)


def image_step(
    part_ref, jump_ref, dir_ref, prev_ref, first_in, second_in, liftt_ref, tlt_ref, nb_ref, bd_ref,
    res_ref, jump0_ref, rim0_ref, v_ref, prev0_ref, coeff_ref, sums_ref, rim, image,
):
    face_dofs = first_in.shape[0]
    elements = dir_ref.shape[1]
    rim_rows = rim.shape[0]
    rim_terms(first_in, second_in, nb_ref, bd_ref, rim, face_dofs, elements)
    image[...] = finish_operator(part_ref, dir_ref, prev_ref, liftt_ref, tlt_ref, rim, face_dofs)
    res, img = res_ref[...], image[...]
    cross = column_sum(res * img)
    square = column_sum(img * img)
    j0 = jnp.concatenate([jump0_ref[:rim_rows, :] + rim0_ref[...], jump0_ref[rim_rows:, :]], axis=0)
    j1 = jnp.concatenate([jump_ref[:rim_rows, :] + rim[...], jump_ref[rim_rows:, :]], axis=0)
    t0 = time_jump_of(v_ref, prev0_ref)
    t1 = time_jump_of(dir_ref, prev_ref)
    bend = square + 0.5 * column_sum(j1 * j1) + column_sum(t1 * t1)
    slope = 0.5 * column_sum(j0 * j1) + column_sum(t0 * t1) - cross
    best = jnp.where(bend > 0.0, -slope / jnp.where(bend > 0.0, bend, 1.0), 0.0)
    r = res - best * img
    j = j0 + best * j1
    t = t0 + best * t1
    base = column_sum(r * r) + 0.5 * column_sum(j * j) + column_sum(t * t)
    tilt = slope + best * bend
    bend_all = total_sum(bend)
    weighted = total_sum(best * bend)
    centre = jnp.where(bend_all > 0.0, weighted / jnp.where(bend_all > 0.0, bend_all, 1.0), 0.0)
    off = centre - best
    base_all = total_sum(base + off * (2.0 * tilt + off * bend))
    tilt_all = total_sum(tilt + off * bend)
    coeff_ref[...] = jnp.concatenate([base, tilt, bend, best, best, best, best, best], axis=0)
    lane = lax.broadcasted_iota(jnp.int32, sums_ref.shape, 1)
    out = jnp.zeros(sums_ref.shape, jnp.float32)
    for i, value in enumerate((total_sum(cross), total_sum(square), base_all, tilt_all, bend_all, centre)):
        out = jnp.where(lane == i, value, out)
    sums_ref[...] = out


def last_step(count, all_ref, coeff_ref, v_ref, dir_ref, smooth_ref, ind_ref, est_ref):
    sums = all_ref[...]
    step = jnp.sum(sums[:, 0:1], axis=0, keepdims=True) / jnp.sum(sums[:, 1:2], axis=0, keepdims=True)
    smooth_ref[...] = v_ref[...] + step * dir_ref[...]
    off = step - sums[:, 5:6]
    total = jnp.sum(sums[:, 2:3] + off * (2.0 * sums[:, 3:4] + off * sums[:, 4:5]), axis=0, keepdims=True)
    delta = step - coeff_ref[3:4, :]
    eta = coeff_ref[0:1, :] + delta * (2.0 * coeff_ref[1:2, :] + delta * coeff_ref[2:3, :])
    ind_ref[...] = eta * count / total
    est_ref[...] = jnp.broadcast_to(jnp.sqrt(total / count), est_ref.shape)


VM = pl.BlockSpec(memory_space=pltpu.VMEM)
HB = pl.BlockSpec(memory_space=pltpu.HBM)


def call(body, name, outs, args, flops, scratch=(), spec=VM):
    shapes = [jax.ShapeDtypeStruct(s, jnp.float32) for s in outs]
    moved = sum(4 * a.size for a in args) + sum(4 * s.size for s in shapes)
    return pl.pallas_call(
        body,
        name=name,
        out_shape=shapes,
        in_specs=[spec] * len(args),
        out_specs=[VM] * len(outs),
        scratch_shapes=[pltpu.VMEM(s, jnp.float32) if isinstance(s, tuple) else s for s in scratch],
        cost_estimate=pl.CostEstimate(flops=flops, bytes_accessed=moved, transcendentals=0),
        compiler_params=pltpu.CompilerParams(vmem_limit_bytes=20 * 2**20),
    )(*args)


def full_swaps(first, slabs, parts):
    other = {i: i + 1 for i in range(first, parts - 1, 2)}
    other.update({j: i for i, j in list(other.items())})
    pairs = []
    for t in range(slabs):
        beside = t ^ 1 if slabs % 2 == 0 else (t + 1) % slabs
        for p in range(parts):
            pairs.append((t * parts + p, t * parts + other[p] if p in other else beside * parts + p))
    return pairs


def on_device(initial, rhs, coef, stiffness, block_inverse, face_proj, lift, time_lift, neighbour, boundary, send_list):
    source = rhs[0]
    dofs, elements = source.shape
    half = time_lift.shape[1]
    traces = face_proj.shape[0]
    face_dofs = traces // 6
    border = send_list.shape[0] // 2
    slabs, parts = lax.axis_size("tm"), lax.axis_size("space")
    devices = slabs * parts
    coef_row = coef.reshape(1, elements)
    send = send_list.reshape(2, border)
    liftt, tlt = lift.T, time_lift.T
    cycle = [(i, (i + 1) % slabs) for i in range(slabs)]

    def halo(a, b):
        swap = lambda x, first: lax.ppermute(x, ("tm", "space"), full_swaps(first, slabs, parts))
        return swap(a, 0), swap(b, 1)

    two = 2 * face_dofs
    v0, end0, tr0, a0, b0 = call(
        first_send,
        "send0",
        [(dofs, elements), (half, elements), (two, elements), (face_dofs, border), (face_dofs, border)],
        (initial[0], face_proj, send),
        2 * two * dofs * elements,
        scratch=[(traces, dofs), pltpu.VMEM(send.shape, send.dtype), pltpu.SemaphoreType.DMA((4,))],
        spec=HB,
    )
    prev0 = lax.ppermute(end0, "tm", cycle)
    a0, b0 = halo(a0, b0)
    local = functools.partial(
        call, local_part, "local", [(dofs, elements), (traces, elements)], flops=12 * traces * dofs * elements, scratch=[(traces, elements)]
    )
    part0, jump0 = local(args=(v0, tr0, coef_row, face_proj, stiffness, liftt, neighbour, boundary))
    res, rim0, direction, end, tr1, a1, b1 = call(
        residual_step,
        "residual",
        [(dofs, elements), (two, elements), (dofs, elements), (half, elements), (two, elements), (face_dofs, border), (face_dofs, border)],
        (part0, v0, source, prev0, a0, b0, coef_row, block_inverse, face_proj, liftt, tlt, neighbour, boundary, send),
        12 * dofs * dofs * elements,
    )
    prev1 = lax.ppermute(end, "tm", cycle)
    a1, b1 = halo(a1, b1)
    part1, jump1 = local(args=(direction, tr1, coef_row, face_proj, stiffness, liftt, neighbour, boundary))
    coeffs, sums = call(
        image_step,
        "image",
        [(SUBS, elements), (devices, LANES)],
        (part1, jump1, direction, prev1, a1, b1, liftt, tlt, neighbour, boundary, res, jump0, rim0, v0, prev0),
        12 * dofs * dofs * elements,
        scratch=[(two, elements), (dofs, elements)],
    )
    everyone = lax.all_to_all(sums, ("tm", "space"), 0, 0, tiled=True)
    smoothed, indicator, estimate = call(
        functools.partial(last_step, float(elements * devices)),
        "last",
        [(dofs, elements), (1, elements), (1, LANES)],
        (everyone, coeffs, v0, direction),
        4 * dofs * elements,
    )
    return smoothed[None], indicator, estimate[0, :1]


def solution(mesh):
    placed = (
        P("tm", None, "space"),
        P("tm", None, "space"),
        P("space"),
        P(),
        P(),
        P(),
        P(),
        P(),
        P(None, "space"),
        P(None, "space"),
        P("space"),
    )
    return jax.shard_map(
        on_device,
        mesh=mesh,
        in_specs=placed,
        out_specs=(P("tm", None, "space"), P("tm", "space"), P()),
        check_vma=False,
    )
```

```python
import functools

import jax
import jax.numpy as jnp
from jax import lax
from jax.experimental import pallas as pl
from jax.experimental.pallas import tpu as pltpu
from jax.sharding import PartitionSpec as P

LANES = 128
SUBS = 8


def dot(a, b):
    return jnp.dot(a, b, precision=lax.Precision.HIGHEST, preferred_element_type=jnp.float32)


def lane_gather(tile_of, tiles, columns, rows):
    shape = (SUBS, LANES)
    low = jnp.broadcast_to(jnp.bitwise_and(columns, LANES - 1), shape)
    high = jnp.broadcast_to(jnp.right_shift(columns, 7), shape)
    found = [jnp.zeros(shape, jnp.float32) for _ in range(rows // SUBS)]
    for tile in range(tiles):
        here = high == tile
        for r in range(rows // SUBS):
            picked = jnp.take_along_axis(tile_of(tile, r), low, axis=1)
            found[r] = jnp.where(here, picked, found[r])
    return found


def face_rows(ref, face, face_dofs):
    return ref[pl.ds(face, face_dofs, stride=6), :]


def is_odd():
    return lax.rem(lax.axis_index("space"), 2) == 1


def fill_outbound(traces, send_ref, first_ref, second_ref, face_dofs, elements):
    per_face = elements // LANES
    odd = is_odd()

    def tile_of(tile, r):
        face, col = divmod(tile, per_face)
        return traces[face * face_dofs + r * SUBS : face * face_dofs + (r + 1) * SUBS, col * LANES : (col + 1) * LANES]

    border = send_ref.shape[1]
    for j in range(border // LANES):
        cols = slice(j * LANES, (j + 1) * LANES)
        lower = lane_gather(tile_of, 2 * per_face, send_ref[0:1, cols], face_dofs)
        upper = lane_gather(tile_of, 2 * per_face, send_ref[1:2, cols], face_dofs)
        for r in range(face_dofs // SUBS):
            rows = slice(r * SUBS, (r + 1) * SUBS)
            first_ref[rows, cols] = jnp.where(odd, lower[r], upper[r])
            second_ref[rows, cols] = jnp.where(odd, upper[r], lower[r])


def fill_jump(traces, nb_ref, bd_ref, jump_ref, face_dofs, elements):
    per_face = elements // LANES
    for face in range(6):
        other = face ^ 1

        def tile_of(tile, r, other=other):
            return traces[other * face_dofs + r * SUBS : other * face_dofs + (r + 1) * SUBS, tile * LANES : (tile + 1) * LANES]

        for j in range(per_face):
            cols = slice(j * LANES, (j + 1) * LANES)
            found = lane_gather(tile_of, per_face, nb_ref[face : face + 1, cols] - other * elements, face_dofs)
            open_face = jnp.broadcast_to(1.0 - bd_ref[face : face + 1, cols].astype(jnp.float32), (SUBS, LANES))
            for r in range(face_dofs // SUBS):
                rows = slice(face * face_dofs + r * SUBS, face * face_dofs + (r + 1) * SUBS)
                jump_ref[rows, cols] = traces[rows, cols] - found[r] * open_face


def rim_terms(first_ref, second_ref, nb_ref, bd_ref, rim_ref, face_dofs, elements):
    tiles = first_ref.shape[1] // LANES
    odd, place, parts = is_odd(), lax.axis_index("space"), lax.axis_size("space")
    sides = []
    for side in range(2):
        for t in range(tiles):
            cols = slice(t * LANES, (t + 1) * LANES)
            a, b = first_ref[:, cols], second_ref[:, cols]
            values = jnp.where(odd, a, b) if side == 0 else jnp.where(odd, b, a)
            there = place > 0 if side == 0 else place < parts - 1
            sides.append(jnp.where(there, values, 0.0))

    def tile_of(tile, r):
        return sides[tile][r * SUBS : (r + 1) * SUBS, :]

    for j in range(elements // LANES):
        cols = slice(j * LANES, (j + 1) * LANES)
        for face in range(2):
            found = lane_gather(tile_of, 2 * tiles, nb_ref[face : face + 1, cols] - 6 * elements, face_dofs)
            open_face = jnp.broadcast_to(1.0 - bd_ref[face : face + 1, cols].astype(jnp.float32), (SUBS, LANES))
            for r in range(face_dofs // SUBS):
                rows = slice(face * face_dofs + r * SUBS, face * face_dofs + (r + 1) * SUBS)
                rim_ref[rows, cols] = 0.0 - found[r] * open_face


def first_send(v_hbm, fp_hbm, send_hbm, v_ref, end_ref, tr_ref, first_ref, second_ref, fp_ref, send_ref, sems):
    face_dofs = fp_ref.shape[0] // 6
    elements = v_ref.shape[1]
    half = end_ref.shape[0]
    pairs = ((v_hbm, v_ref), (fp_hbm, fp_ref), (send_hbm, send_ref), (v_hbm.at[pl.ds(half, half), :], end_ref))
    copies = [pltpu.make_async_copy(a, b, sems.at[i]) for i, (a, b) in enumerate(pairs)]
    for copy in copies:
        copy.start()
    for copy in copies[:3]:
        copy.wait()
    weights = jnp.concatenate([face_rows(fp_ref, f, face_dofs) for f in range(2)], axis=0)
    tr_ref[...] = dot(weights, v_ref[...])
    fill_outbound(tr_ref, send_ref, first_ref, second_ref, face_dofs, elements)
    copies[3].wait()


def local_part(v_ref, tr_ref, coef_ref, fp_ref, stiff_ref, liftt_ref, nb_ref, bd_ref, part_ref, jump_ref, traces):
    face_dofs = fp_ref.shape[0] // 6
    elements = v_ref.shape[1]
    traces[: 2 * face_dofs, :] = tr_ref[...]
    weights = jnp.concatenate([face_rows(fp_ref, f, face_dofs) for f in range(2, 6)], axis=0)
    traces[2 * face_dofs :, :] = dot(weights, v_ref[...])
    fill_jump(traces, nb_ref, bd_ref, jump_ref, face_dofs, elements)
    liftt = jnp.concatenate([face_rows(liftt_ref, f, face_dofs) for f in range(6)], axis=0)
    part_ref[...] = coef_ref[...] * dot(stiff_ref[...], v_ref[...]) + dot(liftt.T, jump_ref[...])


def time_jump_of(v_ref, prev_ref):
    return v_ref[: prev_ref.shape[0], :] - jnp.where(lax.axis_index("tm") > 0, prev_ref[...], 0.0)


def finish_operator(part_ref, v_ref, prev_ref, liftt_ref, tlt_ref, rim, face_dofs):
    time_jump = time_jump_of(v_ref, prev_ref)
    liftt = jnp.concatenate([face_rows(liftt_ref, f, face_dofs) for f in range(2)] + [tlt_ref[...]], axis=0)
    values = jnp.concatenate([rim[...], time_jump], axis=0)
    return part_ref[...] + dot(liftt.T, values)


def residual_step(
    part_ref, v_ref, rhs_ref, prev_ref, first_in, second_in, coef_ref, inv_ref, fp_ref, liftt_ref, tlt_ref,
    nb_ref, bd_ref, send_ref, res_ref, rim_ref, dir_ref, end_ref, tr_ref, first_ref, second_ref,
):
    face_dofs = fp_ref.shape[0] // 6
    elements = v_ref.shape[1]
    half = prev_ref.shape[0]
    rim_terms(first_in, second_in, nb_ref, bd_ref, rim_ref, face_dofs, elements)
    res_ref[...] = rhs_ref[...] - finish_operator(part_ref, v_ref, prev_ref, liftt_ref, tlt_ref, rim_ref, face_dofs)
    direction = dot(inv_ref[...], res_ref[...]) / coef_ref[...]
    dir_ref[...] = direction
    end_ref[...] = direction[half:, :]
    weights = jnp.concatenate([face_rows(fp_ref, f, face_dofs) for f in range(2)], axis=0)
    tr_ref[...] = dot(weights, direction)
    fill_outbound(tr_ref, send_ref, first_ref, second_ref, face_dofs, elements)


def column_sum(x):
    return jnp.sum(x, axis=0, keepdims=True)


def total_sum(row):
    return jnp.sum(row, axis=1, keepdims=True)


def image_step(
    part_ref, jump_ref, dir_ref, prev_ref, first_in, second_in, liftt_ref, tlt_ref, nb_ref, bd_ref,
    res_ref, jump0_ref, rim0_ref, v_ref, prev0_ref, coeff_ref, sums_ref, rim, image,
):
    face_dofs = first_in.shape[0]
    elements = dir_ref.shape[1]
    rim_rows = rim.shape[0]
    rim_terms(first_in, second_in, nb_ref, bd_ref, rim, face_dofs, elements)
    image[...] = finish_operator(part_ref, dir_ref, prev_ref, liftt_ref, tlt_ref, rim, face_dofs)
    res, img = res_ref[...], image[...]
    cross = column_sum(res * img)
    square = column_sum(img * img)
    j0 = jnp.concatenate([jump0_ref[:rim_rows, :] + rim0_ref[...], jump0_ref[rim_rows:, :]], axis=0)
    j1 = jnp.concatenate([jump_ref[:rim_rows, :] + rim[...], jump_ref[rim_rows:, :]], axis=0)
    t0 = time_jump_of(v_ref, prev0_ref)
    t1 = time_jump_of(dir_ref, prev_ref)
    bend = square + 0.5 * column_sum(j1 * j1) + column_sum(t1 * t1)
    slope = 0.5 * column_sum(j0 * j1) + column_sum(t0 * t1) - cross
    best = jnp.where(bend > 0.0, -slope / jnp.where(bend > 0.0, bend, 1.0), 0.0)
    r = res - best * img
    j = j0 + best * j1
    t = t0 + best * t1
    base = column_sum(r * r) + 0.5 * column_sum(j * j) + column_sum(t * t)
    tilt = slope + best * bend
    bend_all = total_sum(bend)
    weighted = total_sum(best * bend)
    centre = jnp.where(bend_all > 0.0, weighted / jnp.where(bend_all > 0.0, bend_all, 1.0), 0.0)
    off = centre - best
    base_all = total_sum(base + off * (2.0 * tilt + off * bend))
    tilt_all = total_sum(tilt + off * bend)
    coeff_ref[...] = jnp.concatenate([base, tilt, bend, best, best, best, best, best], axis=0)
    lane = lax.broadcasted_iota(jnp.int32, sums_ref.shape, 1)
    out = jnp.zeros(sums_ref.shape, jnp.float32)
    for i, value in enumerate((total_sum(cross), total_sum(square), base_all, tilt_all, bend_all, centre)):
        out = jnp.where(lane == i, value, out)
    sums_ref[...] = out


def last_step(count, all_ref, coeff_ref, v_ref, dir_ref, smooth_ref, ind_ref, est_ref):
    sums = all_ref[...]
    step = jnp.sum(sums[:, 0:1], axis=0, keepdims=True) / jnp.sum(sums[:, 1:2], axis=0, keepdims=True)
    smooth_ref[...] = v_ref[...] + step * dir_ref[...]
    off = step - sums[:, 5:6]
    total = jnp.sum(sums[:, 2:3] + off * (2.0 * sums[:, 3:4] + off * sums[:, 4:5]), axis=0, keepdims=True)
    delta = step - coeff_ref[3:4, :]
    eta = coeff_ref[0:1, :] + delta * (2.0 * coeff_ref[1:2, :] + delta * coeff_ref[2:3, :])
    ind_ref[...] = eta * count / total
    est_ref[...] = jnp.broadcast_to(jnp.sqrt(total / count), est_ref.shape)


VM = pl.BlockSpec(memory_space=pltpu.VMEM)
HB = pl.BlockSpec(memory_space=pltpu.HBM)


def call(body, name, outs, args, flops, scratch=(), spec=VM):
    shapes = [jax.ShapeDtypeStruct(s, jnp.float32) for s in outs]
    moved = sum(4 * a.size for a in args) + sum(4 * s.size for s in shapes)
    return pl.pallas_call(
        body,
        name=name,
        out_shape=shapes,
        in_specs=[spec] * len(args),
        out_specs=[VM] * len(outs),
        scratch_shapes=[pltpu.VMEM(s, jnp.float32) if isinstance(s, tuple) else s for s in scratch],
        cost_estimate=pl.CostEstimate(flops=flops, bytes_accessed=moved, transcendentals=0),
        compiler_params=pltpu.CompilerParams(vmem_limit_bytes=20 * 2**20),
    )(*args)


def full_swaps(first, slabs, parts):
    other = {i: i + 1 for i in range(first, parts - 1, 2)}
    other.update({j: i for i, j in list(other.items())})
    pairs = []
    for t in range(slabs):
        beside = t ^ 1 if slabs % 2 == 0 else (t + 1) % slabs
        for p in range(parts):
            pairs.append((t * parts + p, t * parts + other[p] if p in other else beside * parts + p))
    return pairs


def on_device(initial, rhs, coef, stiffness, block_inverse, face_proj, lift, time_lift, neighbour, boundary, send_list):
    source = rhs[0]
    dofs, elements = source.shape
    half = time_lift.shape[1]
    traces = face_proj.shape[0]
    face_dofs = traces // 6
    border = send_list.shape[0] // 2
    slabs, parts = lax.axis_size("tm"), lax.axis_size("space")
    devices = slabs * parts
    coef_row = coef.reshape(1, elements)
    send = send_list.reshape(2, border)
    liftt, tlt = lift.T, time_lift.T
    cycle = [(i, (i + 1) % slabs) for i in range(slabs)]

    def halo(a, b):
        swap = lambda x, first: lax.ppermute(x, ("tm", "space"), full_swaps(first, slabs, parts))
        return swap(a, 0), swap(b, 1)

    two = 2 * face_dofs
    v0, end0, tr0, a0, b0 = call(
        first_send,
        "send0",
        [(dofs, elements), (half, elements), (two, elements), (face_dofs, border), (face_dofs, border)],
        tuple(pltpu.with_memory_space_constraint(x, pltpu.HBM) for x in (initial[0], face_proj, send)),
        2 * two * dofs * elements,
        scratch=[(traces, dofs), pltpu.VMEM(send.shape, send.dtype), pltpu.SemaphoreType.DMA((4,))],
        spec=HB,
    )
    prev0 = lax.ppermute(end0, "tm", cycle)
    a0, b0 = halo(a0, b0)
    local = functools.partial(
        call, local_part, "local", [(dofs, elements), (traces, elements)], flops=12 * traces * dofs * elements, scratch=[(traces, elements)]
    )
    part0, jump0 = local(args=(v0, tr0, coef_row, face_proj, stiffness, liftt, neighbour, boundary))
    res, rim0, direction, end, tr1, a1, b1 = call(
        residual_step,
        "residual",
        [(dofs, elements), (two, elements), (dofs, elements), (half, elements), (two, elements), (face_dofs, border), (face_dofs, border)],
        (part0, v0, source, prev0, a0, b0, coef_row, block_inverse, face_proj, liftt, tlt, neighbour, boundary, send),
        12 * dofs * dofs * elements,
    )
    prev1 = lax.ppermute(end, "tm", cycle)
    a1, b1 = halo(a1, b1)
    part1, jump1 = local(args=(direction, tr1, coef_row, face_proj, stiffness, liftt, neighbour, boundary))
    coeffs, sums = call(
        image_step,
        "image",
        [(SUBS, elements), (devices, LANES)],
        (part1, jump1, direction, prev1, a1, b1, liftt, tlt, neighbour, boundary, res, jump0, rim0, v0, prev0),
        12 * dofs * dofs * elements,
        scratch=[(two, elements), (dofs, elements)],
    )
    everyone = lax.all_to_all(sums, ("tm", "space"), 0, 0, tiled=True)
    smoothed, indicator, estimate = call(
        functools.partial(last_step, float(elements * devices)),
        "last",
        [(dofs, elements), (1, elements), (1, LANES)],
        (everyone, coeffs, v0, direction),
        4 * dofs * elements,
    )
    return smoothed[None], indicator, estimate[0, :1]


def solution(mesh):
    placed = (
        P("tm", None, "space"),
        P("tm", None, "space"),
        P("space"),
        P(),
        P(),
        P(),
        P(),
        P(),
        P(None, "space"),
        P(None, "space"),
        P("space"),
    )
    return jax.shard_map(
        on_device,
        mesh=mesh,
        in_specs=placed,
        out_specs=(P("tm", None, "space"), P("tm", "space"), P()),
        check_vma=False,
    )
```

```python
import functools

import jax
import jax.numpy as jnp
from jax import lax
from jax.experimental import pallas as pl
from jax.experimental.pallas import tpu as pltpu
from jax.sharding import PartitionSpec as P

LANES = 128
SUBS = 8


WIDE = 256


def dot(a, b):
    return jnp.dot(a, b, precision=lax.Precision.HIGHEST, preferred_element_type=jnp.float32)


def split(x):
    high = x.astype(jnp.bfloat16)
    return high, (x - high.astype(jnp.float32)).astype(jnp.bfloat16)


def left3(w):
    high, low = split(w)
    return jnp.concatenate([high, low, high], axis=1)


def dot3(w3, x):
    high, low = split(x)
    return jnp.dot(w3, jnp.concatenate([high, high, low], axis=0), preferred_element_type=jnp.float32)


def chunks(elements):
    width = WIDE if elements % WIDE == 0 else LANES
    return [slice(c, c + width) for c in range(0, elements, width)]


def lane_gather(tile_of, tiles, columns, rows):
    shape = (SUBS, LANES)
    low = jnp.broadcast_to(jnp.bitwise_and(columns, LANES - 1), shape)
    high = jnp.broadcast_to(jnp.right_shift(columns, 7), shape)
    found = [jnp.zeros(shape, jnp.float32) for _ in range(rows // SUBS)]
    for tile in range(tiles):
        here = high == tile
        for r in range(rows // SUBS):
            picked = jnp.take_along_axis(tile_of(tile, r), low, axis=1)
            found[r] = jnp.where(here, picked, found[r])
    return found


def face_rows(ref, face, face_dofs):
    return ref[pl.ds(face, face_dofs, stride=6), :]


def is_odd():
    return lax.rem(lax.axis_index("space"), 2) == 1


def fill_outbound(traces, send_ref, first_ref, second_ref, face_dofs, elements):
    per_face = elements // LANES
    odd = is_odd()

    def tile_of(tile, r):
        face, col = divmod(tile, per_face)
        return traces[face * face_dofs + r * SUBS : face * face_dofs + (r + 1) * SUBS, col * LANES : (col + 1) * LANES]

    border = send_ref.shape[1]
    for j in range(border // LANES):
        cols = slice(j * LANES, (j + 1) * LANES)
        lower = lane_gather(tile_of, 2 * per_face, send_ref[0:1, cols], face_dofs)
        upper = lane_gather(tile_of, 2 * per_face, send_ref[1:2, cols], face_dofs)
        for r in range(face_dofs // SUBS):
            rows = slice(r * SUBS, (r + 1) * SUBS)
            first_ref[rows, cols] = jnp.where(odd, lower[r], upper[r])
            second_ref[rows, cols] = jnp.where(odd, upper[r], lower[r])


def fill_jump(traces, nb_ref, bd_ref, jump_ref, face_dofs, elements):
    per_face = elements // LANES
    for face in range(6):
        other = face ^ 1

        def tile_of(tile, r, other=other):
            return traces[other * face_dofs + r * SUBS : other * face_dofs + (r + 1) * SUBS, tile * LANES : (tile + 1) * LANES]

        for j in range(per_face):
            cols = slice(j * LANES, (j + 1) * LANES)
            found = lane_gather(tile_of, per_face, nb_ref[face : face + 1, cols] - other * elements, face_dofs)
            open_face = jnp.broadcast_to(1.0 - bd_ref[face : face + 1, cols].astype(jnp.float32), (SUBS, LANES))
            for r in range(face_dofs // SUBS):
                rows = slice(face * face_dofs + r * SUBS, face * face_dofs + (r + 1) * SUBS)
                jump_ref[rows, cols] = traces[rows, cols] - found[r] * open_face


def rim_terms(first_ref, second_ref, nb_ref, bd_ref, rim_ref, face_dofs, elements):
    tiles = first_ref.shape[1] // LANES
    odd, place, parts = is_odd(), lax.axis_index("space"), lax.axis_size("space")
    sides = []
    for side in range(2):
        for t in range(tiles):
            cols = slice(t * LANES, (t + 1) * LANES)
            a, b = first_ref[:, cols], second_ref[:, cols]
            values = jnp.where(odd, a, b) if side == 0 else jnp.where(odd, b, a)
            there = place > 0 if side == 0 else place < parts - 1
            sides.append(jnp.where(there, values, 0.0))

    def tile_of(tile, r):
        return sides[tile][r * SUBS : (r + 1) * SUBS, :]

    for j in range(elements // LANES):
        cols = slice(j * LANES, (j + 1) * LANES)
        for face in range(2):
            found = lane_gather(tile_of, 2 * tiles, nb_ref[face : face + 1, cols] - 6 * elements, face_dofs)
            open_face = jnp.broadcast_to(1.0 - bd_ref[face : face + 1, cols].astype(jnp.float32), (SUBS, LANES))
            for r in range(face_dofs // SUBS):
                rows = slice(face * face_dofs + r * SUBS, face * face_dofs + (r + 1) * SUBS)
                rim_ref[rows, cols] = 0.0 - found[r] * open_face


def first_send(
    v_hbm, fp_hbm, send_hbm, coef_hbm, nb_hbm, bd_hbm,
    v_ref, end_ref, fp_ref, send_ref, coef_ref, nb_ref, bd_ref, tr_ref, first_ref, second_ref, sems,
):
    face_dofs = fp_ref.shape[0] // 6
    elements = v_ref.shape[1]
    half = end_ref.shape[0]
    parts = chunks(elements)
    pairs = [(fp_hbm, fp_ref)] + [(v_hbm.at[:, c], v_ref.at[:, c]) for c in parts]
    pairs += [(send_hbm, send_ref), (v_hbm.at[pl.ds(half, half), :], end_ref), (coef_hbm, coef_ref), (nb_hbm, nb_ref), (bd_hbm, bd_ref)]
    copies = [pltpu.make_async_copy(a, b, sems.at[i]) for i, (a, b) in enumerate(pairs)]
    for copy in copies:
        copy.start()
    copies[0].wait()
    weights = left3(jnp.concatenate([face_rows(fp_ref, f, face_dofs) for f in range(2)], axis=0))
    for i, c in enumerate(parts):
        copies[1 + i].wait()
        tr_ref[:, c] = dot3(weights, v_ref[:, c])
    copies[1 + len(parts)].wait()
    fill_outbound(tr_ref, send_ref, first_ref, second_ref, face_dofs, elements)
    for copy in copies[2 + len(parts) :]:
        copy.wait()


def all_traces(v_ref, tr_ref, weights, traces):
    known = tr_ref.shape[0]
    for c in chunks(v_ref.shape[1]):
        traces[:known, c] = tr_ref[:, c]
        traces[known:, c] = dot3(weights, v_ref[:, c])


def local_first(
    v_ref, tr_ref, coef_ref, fp_ref, nb_ref, bd_ref, rhs_hbm, stiff_hbm, inv_hbm, liftt_hbm, tlt_hbm,
    jump_ref, part_ref, ahead_ref, fp3_ref, apply3_ref, late3_ref, ahead3_ref,
    traces, rhs, stiff, inv, liftt, tlt, sems,
):
    face_dofs = fp_ref.shape[0] // 6
    elements = v_ref.shape[1]
    pairs = ((stiff_hbm, stiff), (liftt_hbm, liftt), (tlt_hbm, tlt), (inv_hbm, inv), (rhs_hbm, rhs))
    copies = [pltpu.make_async_copy(a, b, sems.at[i]) for i, (a, b) in enumerate(pairs)]
    for copy in copies:
        copy.start()
    fp3_ref[...] = left3(jnp.concatenate([face_rows(fp_ref, f, face_dofs) for f in range(2, 6)], axis=0))
    all_traces(v_ref, tr_ref, fp3_ref[...], traces)
    for copy in copies:
        copy.wait()
    lift_rows = [face_rows(liftt, f, face_dofs) for f in range(6)]
    apply3_ref[...] = left3(jnp.concatenate([stiff[...], jnp.concatenate(lift_rows, axis=0).T], axis=1))
    late = jnp.concatenate(lift_rows[:2] + [tlt[...]], axis=0).T
    late3_ref[...] = left3(late)
    inverse = inv[...]
    first_faces = jnp.concatenate([face_rows(fp_ref, f, face_dofs) for f in range(2)], axis=0)
    both = jnp.concatenate([inverse, dot(first_faces, inverse)], axis=0)
    ahead3_ref[...] = left3(dot(both, late))
    both = left3(both)
    fill_jump(traces, nb_ref, bd_ref, jump_ref, face_dofs, elements)
    for c in chunks(elements):
        values = jnp.concatenate([coef_ref[:, c] * v_ref[:, c], jump_ref[:, c]], axis=0)
        part = rhs[:, c] - dot3(apply3_ref[...], values)
        part_ref[:, c] = part
        ahead_ref[:, c] = dot3(both, part)


def residual_step(
    ahead_ref, v_ref, prev_ref, first_in, second_in, ahead3_ref, coef_ref, nb_ref, bd_ref, send_ref,
    late_ref, dir_ref, end_ref, tr_ref, first_ref, second_ref,
):
    face_dofs = first_in.shape[0]
    dofs, elements = dir_ref.shape
    half = prev_ref.shape[0]
    rim_terms(first_in, second_in, nb_ref, bd_ref, late_ref, face_dofs, elements)
    late_ref[2 * face_dofs :, :] = time_jump_of(v_ref, prev_ref)
    for c in chunks(elements):
        both = (ahead_ref[:, c] - dot3(ahead3_ref[...], late_ref[:, c])) * (1.0 / coef_ref[:, c])
        dir_ref[:, c] = both[:dofs, :]
        end_ref[:, c] = both[half:dofs, :]
        tr_ref[:, c] = both[dofs:, :]
    fill_outbound(tr_ref, send_ref, first_ref, second_ref, face_dofs, elements)


def time_jump_of(v_ref, prev_ref):
    return v_ref[: prev_ref.shape[0], :] - jnp.where(lax.axis_index("tm") > 0, prev_ref[...], 0.0)


def column_sum(x):
    return jnp.sum(x, axis=0, keepdims=True)


def total_sum(row):
    return jnp.sum(row, axis=1, keepdims=True)


def lowest(slope, bend):
    return jnp.where(bend > 0.0, -slope / jnp.where(bend > 0.0, bend, 1.0), 0.0)


def local_second(
    dir_ref, tr_ref, coef_ref, nb_ref, bd_ref, fp3_ref, apply3_ref, late3_ref, part_ref, late_ref, jump0_ref,
    image_ref, border_ref, res_ref, border0_ref, group_ref, traces, jump,
):
    elements = dir_ref.shape[1]
    face_dofs = jump.shape[0] // 6
    rim = 2 * face_dofs
    all_traces(dir_ref, tr_ref, fp3_ref[...], traces)
    fill_jump(traces, nb_ref, bd_ref, jump, face_dofs, elements)
    for c in chunks(elements):
        values = jnp.concatenate([coef_ref[:, c] * dir_ref[:, c], jump[:, c]], axis=0)
        image_ref[:, c] = dot3(apply3_ref[...], values)
        res_ref[:, c] = part_ref[:, c] - dot3(late3_ref[...], late_ref[:, c])
        border_ref[:, c] = jump[:rim, c]
        border0_ref[:, c] = jump0_ref[:rim, c] + late_ref[:rim, c]
        j0, j1 = jump0_ref[rim:, c], jump[rim:, c]
        bend, slope = 0.5 * column_sum(j1 * j1), 0.5 * column_sum(j0 * j1)
        best = lowest(slope, bend)
        j = j0 + best * j1
        base = 0.5 * column_sum(j * j)
        group_ref[:, c] = jnp.concatenate([base, slope, bend, best, base, base, base, base], axis=0)


def image_step(
    part_ref, border_ref, dir_ref, prev_ref, first_in, second_in, late3_ref, nb_ref, bd_ref, res_ref, border0_ref, late0_ref, group_ref,
    coeff_ref, sums_ref, late,
):
    face_dofs = first_in.shape[0]
    elements = dir_ref.shape[1]
    rim = 2 * face_dofs
    rim_terms(first_in, second_in, nb_ref, bd_ref, late, face_dofs, elements)
    late[rim:, :] = time_jump_of(dir_ref, prev_ref)
    crosses, squares = [], []
    for c in chunks(elements):
        img = part_ref[:, c] + dot3(late3_ref[...], late[:, c])
        res = res_ref[:, c]
        cross, square = column_sum(res * img), column_sum(img * img)
        j0, j1 = border0_ref[:, c], border_ref[:, c] + late[:rim, c]
        t0, t1 = late0_ref[rim:, c], late[rim:, c]
        g_base, g_slope, g_bend, g_best = (group_ref[i : i + 1, c] for i in range(4))
        bend = square + 0.5 * column_sum(j1 * j1) + column_sum(t1 * t1) + g_bend
        slope = 0.5 * column_sum(j0 * j1) + column_sum(t0 * t1) + g_slope - cross
        best = lowest(slope, bend)
        r = res - best * img
        j = j0 + best * j1
        t = t0 + best * t1
        off = best - g_best
        group = g_base + off * (2.0 * (g_slope + g_best * g_bend) + off * g_bend)
        base = column_sum(r * r) + 0.5 * column_sum(j * j) + column_sum(t * t) + group
        tilt = slope + best * bend
        coeff_ref[:, c] = jnp.concatenate([base, tilt, bend, best, best, best, best, best], axis=0)
        crosses.append(cross)
        squares.append(square)
    base, tilt, bend, best = (coeff_ref[i : i + 1, :] for i in range(4))
    bend_all = total_sum(bend)
    centre = lowest(-total_sum(best * bend), bend_all)
    off = centre - best
    base_all = total_sum(base + off * (2.0 * tilt + off * bend))
    tilt_all = total_sum(tilt + off * bend)
    cross_all = total_sum(jnp.concatenate(crosses, axis=1))
    square_all = total_sum(jnp.concatenate(squares, axis=1))
    lane = lax.broadcasted_iota(jnp.int32, sums_ref.shape, 1)
    out = jnp.zeros(sums_ref.shape, jnp.float32)
    for i, value in enumerate((cross_all, square_all, base_all, tilt_all, bend_all, centre)):
        out = jnp.where(lane == i, value, out)
    sums_ref[...] = out


def last_step(count, all_ref, coeff_ref, v_ref, dir_ref, smooth_ref, ind_ref, est_ref):
    sums = all_ref[...]
    step = jnp.sum(sums[:, 0:1], axis=0, keepdims=True) / jnp.sum(sums[:, 1:2], axis=0, keepdims=True)
    smooth_ref[...] = v_ref[...] + step * dir_ref[...]
    off = step - sums[:, 5:6]
    total = jnp.sum(sums[:, 2:3] + off * (2.0 * sums[:, 3:4] + off * sums[:, 4:5]), axis=0, keepdims=True)
    delta = step - coeff_ref[3:4, :]
    eta = coeff_ref[0:1, :] + delta * (2.0 * coeff_ref[1:2, :] + delta * coeff_ref[2:3, :])
    ind_ref[...] = eta * count / total
    est_ref[...] = jnp.broadcast_to(jnp.sqrt(total / count), est_ref.shape)


VM = pl.BlockSpec(memory_space=pltpu.VMEM)
HB = pl.BlockSpec(memory_space=pltpu.HBM)
F32, BF16 = jnp.float32, jnp.bfloat16


def call(body, name, outs, args, flops, far=(), scratch=()):
    shapes = [jax.ShapeDtypeStruct(*s) if isinstance(s[0], tuple) else jax.ShapeDtypeStruct(s, F32) for s in outs]
    far = tuple(pltpu.with_memory_space_constraint(x, pltpu.HBM) for x in far)
    moved = sum(4 * a.size for a in args + far) + sum(4 * s.size for s in shapes)
    return pl.pallas_call(
        body,
        name=name,
        out_shape=shapes,
        in_specs=[VM] * len(args) + [HB] * len(far),
        out_specs=[VM] * len(outs),
        scratch_shapes=[pltpu.VMEM(s, F32) if isinstance(s, tuple) else s for s in scratch],
        cost_estimate=pl.CostEstimate(flops=flops, bytes_accessed=moved, transcendentals=0),
        compiler_params=pltpu.CompilerParams(vmem_limit_bytes=24 * 2**20),
    )(*args, *far)


def full_swaps(first, slabs, parts):
    other = {i: i + 1 for i in range(first, parts - 1, 2)}
    other.update({j: i for i, j in list(other.items())})
    pairs = []
    for t in range(slabs):
        beside = t ^ 1 if slabs % 2 == 0 else (t + 1) % slabs
        for p in range(parts):
            pairs.append((t * parts + p, t * parts + other[p] if p in other else beside * parts + p))
    return pairs


def on_device(initial, rhs, coef, stiffness, block_inverse, face_proj, lift, time_lift, neighbour, boundary, send_list):
    source = rhs[0]
    dofs, elements = source.shape
    half = time_lift.shape[1]
    traces = face_proj.shape[0]
    face_dofs = traces // 6
    border = send_list.shape[0] // 2
    slabs, parts = lax.axis_size("tm"), lax.axis_size("space")
    devices = slabs * parts
    coef_row = coef.reshape(1, elements)
    send = send_list.reshape(2, border)
    liftt, tlt = lift.T, time_lift.T
    cycle = [(i, (i + 1) % slabs) for i in range(slabs)]

    def halo(a, b):
        swap = lambda x, first: lax.ppermute(x, ("tm", "space"), full_swaps(first, slabs, parts))
        return swap(a, 0), swap(b, 1)

    rim = 2 * face_dofs
    late = rim + half
    edge = (face_dofs, border)
    v0, end0, fp, send, coefs, nb, bd, tr0, a0, b0 = call(
        first_send,
        "send0",
        [(dofs, elements), (half, elements), (traces, dofs), (send.shape, send.dtype), coef_row.shape]
        + [(neighbour.shape, neighbour.dtype), (boundary.shape, boundary.dtype), (rim, elements), edge, edge],
        (),
        2 * rim * dofs * elements,
        far=(initial[0], face_proj, send, coef_row, neighbour, boundary),
        scratch=[pltpu.SemaphoreType.DMA((6 + len(chunks(elements)),))],
    )
    prev0 = lax.ppermute(end0, "tm", cycle)
    a0, b0 = halo(a0, b0)
    jump0, part0, ahead, fp3, apply3, late3, ahead3 = call(
        local_first,
        "local0",
        [(traces, elements), (dofs, elements), (dofs + rim, elements), ((traces - rim, 3 * dofs), BF16)]
        + [((dofs, 3 * (dofs + traces)), BF16), ((dofs, 3 * late), BF16), ((dofs + rim, 3 * late), BF16)],
        (v0, tr0, coefs, fp, nb, bd),
        12 * traces * dofs * elements,
        far=(source, stiffness, block_inverse, liftt, tlt),
        scratch=[(traces, elements), (dofs, elements), (dofs, dofs), (dofs, dofs), (traces, dofs), (half, dofs), pltpu.SemaphoreType.DMA((5,))],
    )
    late0, direction, end, tr1, a1, b1 = call(
        residual_step,
        "residual",
        [(late, elements), (dofs, elements), (half, elements), (rim, elements), edge, edge],
        (ahead, v0, prev0, a0, b0, ahead3, coefs, nb, bd, send),
        6 * dofs * dofs * elements,
    )
    prev1 = lax.ppermute(end, "tm", cycle)
    a1, b1 = halo(a1, b1)
    part1, border1, res, border0, group = call(
        local_second,
        "local1",
        [(dofs, elements), (rim, elements), (dofs, elements), (rim, elements), (SUBS, elements)],
        (direction, tr1, coefs, nb, bd, fp3, apply3, late3, part0, late0, jump0),
        12 * traces * dofs * elements,
        scratch=[(traces, elements), (traces, elements)],
    )
    coeffs, sums = call(
        image_step,
        "image",
        [(SUBS, elements), (devices, LANES)],
        (part1, border1, direction, prev1, a1, b1, late3, nb, bd, res, border0, late0, group),
        6 * dofs * dofs * elements,
        scratch=[(late, elements)],
    )
    everyone = lax.all_to_all(sums, ("tm", "space"), 0, 0, tiled=True)
    smoothed, indicator, estimate = call(
        functools.partial(last_step, float(elements * devices)),
        "last",
        [(dofs, elements), (1, elements), (1, LANES)],
        (everyone, coeffs, v0, direction),
        4 * dofs * elements,
    )
    return smoothed[None], indicator, estimate[0, :1]


def solution(mesh):
    placed = (
        P("tm", None, "space"),
        P("tm", None, "space"),
        P("space"),
        P(),
        P(),
        P(),
        P(),
        P(),
        P(None, "space"),
        P(None, "space"),
        P("space"),
    )
    return jax.shard_map(
        on_device,
        mesh=mesh,
        in_specs=placed,
        out_specs=(P("tm", None, "space"), P("tm", "space"), P()),
        check_vma=False,
    )
```

```python
import functools

import jax
import jax.numpy as jnp
from jax import lax
from jax.experimental import pallas as pl
from jax.experimental.pallas import tpu as pltpu
from jax.sharding import PartitionSpec as P

LANES = 128
SUBS = 8


WIDE = 256


def dot(a, b):
    return jnp.dot(a, b, precision=lax.Precision.HIGHEST, preferred_element_type=jnp.float32)


def split(x):
    high = x.astype(jnp.bfloat16)
    return high, (x - high.astype(jnp.float32)).astype(jnp.bfloat16)


def left3(w):
    high, low = split(w)
    return jnp.concatenate([high, low, high], axis=1)


def dot3(w3, x):
    high, low = split(x)
    return jnp.dot(w3, jnp.concatenate([high, high, low], axis=0), preferred_element_type=jnp.float32)


def chunks(elements):
    width = WIDE if elements % WIDE == 0 else LANES
    return [slice(c, c + width) for c in range(0, elements, width)]


def lane_gather(tile_of, tiles, columns, rows):
    shape = (SUBS, LANES)
    low = jnp.broadcast_to(jnp.bitwise_and(columns, LANES - 1), shape)
    high = jnp.broadcast_to(jnp.right_shift(columns, 7), shape)
    found = [jnp.zeros(shape, jnp.float32) for _ in range(rows // SUBS)]
    for tile in range(tiles):
        here = high == tile
        for r in range(rows // SUBS):
            picked = jnp.take_along_axis(tile_of(tile, r), low, axis=1)
            found[r] = jnp.where(here, picked, found[r])
    return found


def face_rows(ref, face, face_dofs):
    return ref[pl.ds(face, face_dofs, stride=6), :]


def is_odd():
    return lax.rem(lax.axis_index("space"), 2) == 1


def fill_outbound(traces, send_ref, first_ref, second_ref, face_dofs, elements):
    per_face = elements // LANES
    odd = is_odd()

    def tile_of(tile, r):
        face, col = divmod(tile, per_face)
        return traces[face * face_dofs + r * SUBS : face * face_dofs + (r + 1) * SUBS, col * LANES : (col + 1) * LANES]

    border = send_ref.shape[1]
    for j in range(border // LANES):
        cols = slice(j * LANES, (j + 1) * LANES)
        lower = lane_gather(tile_of, 2 * per_face, send_ref[0:1, cols], face_dofs)
        upper = lane_gather(tile_of, 2 * per_face, send_ref[1:2, cols], face_dofs)
        for r in range(face_dofs // SUBS):
            rows = slice(r * SUBS, (r + 1) * SUBS)
            first_ref[rows, cols] = jnp.where(odd, lower[r], upper[r])
            second_ref[rows, cols] = jnp.where(odd, upper[r], lower[r])


def fill_jump(traces, nb_ref, bd_ref, jump_ref, face_dofs, elements, chunk):
    per_face = elements // LANES
    for face in range(6):
        other = face ^ 1

        def tile_of(tile, r, other=other):
            return traces[other * face_dofs + r * SUBS : other * face_dofs + (r + 1) * SUBS, tile * LANES : (tile + 1) * LANES]

        for start in range(chunk.start, chunk.stop, LANES):
            cols = slice(start, start + LANES)
            found = lane_gather(tile_of, per_face, nb_ref[face : face + 1, cols] - other * elements, face_dofs)
            open_face = jnp.broadcast_to(1.0 - bd_ref[face : face + 1, cols].astype(jnp.float32), (SUBS, LANES))
            for r in range(face_dofs // SUBS):
                rows = slice(face * face_dofs + r * SUBS, face * face_dofs + (r + 1) * SUBS)
                jump_ref[rows, cols] = traces[rows, cols] - found[r] * open_face


def rim_terms(first_ref, second_ref, nb_ref, bd_ref, rim_ref, face_dofs, elements):
    tiles = first_ref.shape[1] // LANES
    odd, place, parts = is_odd(), lax.axis_index("space"), lax.axis_size("space")
    sides = []
    for side in range(2):
        for t in range(tiles):
            cols = slice(t * LANES, (t + 1) * LANES)
            a, b = first_ref[:, cols], second_ref[:, cols]
            values = jnp.where(odd, a, b) if side == 0 else jnp.where(odd, b, a)
            there = place > 0 if side == 0 else place < parts - 1
            sides.append(jnp.where(there, values, 0.0))

    def tile_of(tile, r):
        return sides[tile][r * SUBS : (r + 1) * SUBS, :]

    for j in range(elements // LANES):
        cols = slice(j * LANES, (j + 1) * LANES)
        for face in range(2):
            found = lane_gather(tile_of, 2 * tiles, nb_ref[face : face + 1, cols] - 6 * elements, face_dofs)
            open_face = jnp.broadcast_to(1.0 - bd_ref[face : face + 1, cols].astype(jnp.float32), (SUBS, LANES))
            for r in range(face_dofs // SUBS):
                rows = slice(face * face_dofs + r * SUBS, face * face_dofs + (r + 1) * SUBS)
                rim_ref[rows, cols] = 0.0 - found[r] * open_face


def first_send(
    v_hbm, fp_hbm, send_hbm, coef_hbm, nb_hbm, bd_hbm,
    v_ref, end_ref, fp_ref, send_ref, coef_ref, nb_ref, bd_ref, tr_ref, first_ref, second_ref, sems,
):
    face_dofs = fp_ref.shape[0] // 6
    elements = v_ref.shape[1]
    half = end_ref.shape[0]
    parts = chunks(elements)
    pairs = [(fp_hbm, fp_ref)] + [(v_hbm.at[:, c], v_ref.at[:, c]) for c in parts]
    pairs += [(send_hbm, send_ref), (coef_hbm, coef_ref), (nb_hbm, nb_ref), (bd_hbm, bd_ref)]
    copies = [pltpu.make_async_copy(a, b, sems.at[i]) for i, (a, b) in enumerate(pairs)]
    for copy in copies:
        copy.start()
    copies[0].wait()
    weights = left3(jnp.concatenate([face_rows(fp_ref, f, face_dofs) for f in range(2)], axis=0))
    for i, c in enumerate(parts):
        copies[1 + i].wait()
        tr_ref[:, c] = dot3(weights, v_ref[:, c])
        end_ref[:, c] = v_ref[half:, c]
    copies[1 + len(parts)].wait()
    fill_outbound(tr_ref, send_ref, first_ref, second_ref, face_dofs, elements)
    for copy in copies[2 + len(parts) :]:
        copy.wait()


def all_traces(v_ref, tr_ref, weights, traces):
    known = tr_ref.shape[0]
    for c in chunks(v_ref.shape[1]):
        traces[:known, c] = tr_ref[:, c]
        traces[known:, c] = dot3(weights, v_ref[:, c])


def local_first(
    v_ref, tr_ref, coef_ref, fp_ref, nb_ref, bd_ref, rhs_hbm, stiff_hbm, inv_hbm, liftt_hbm, tlt_hbm,
    jump_ref, part_ref, ahead_ref, fp3_ref, apply3_ref, late3_ref, ahead3_ref,
    traces, rhs, stiff, inv, liftt, tlt, sems,
):
    face_dofs = fp_ref.shape[0] // 6
    elements = v_ref.shape[1]
    pairs = ((stiff_hbm, stiff), (liftt_hbm, liftt), (tlt_hbm, tlt), (inv_hbm, inv), (rhs_hbm, rhs))
    copies = [pltpu.make_async_copy(a, b, sems.at[i]) for i, (a, b) in enumerate(pairs)]
    for copy in copies:
        copy.start()
    fp3_ref[...] = left3(jnp.concatenate([face_rows(fp_ref, f, face_dofs) for f in range(2, 6)], axis=0))
    all_traces(v_ref, tr_ref, fp3_ref[...], traces)
    parts = chunks(elements)
    early = (len(parts) + 1) // 2
    for c in parts[:early]:
        fill_jump(traces, nb_ref, bd_ref, jump_ref, face_dofs, elements, c)
    for copy in copies:
        copy.wait()
    lift_rows = [face_rows(liftt, f, face_dofs) for f in range(6)]
    apply3_ref[...] = left3(jnp.concatenate([stiff[...], jnp.concatenate(lift_rows, axis=0).T], axis=1))
    late = jnp.concatenate(lift_rows[:2] + [tlt[...]], axis=0).T
    late3_ref[...] = left3(late)
    inverse = inv[...]
    first_faces = jnp.concatenate([face_rows(fp_ref, f, face_dofs) for f in range(2)], axis=0)
    both = jnp.concatenate([inverse, dot(first_faces, inverse)], axis=0)
    ahead3_ref[...] = left3(dot(both, late))
    both = left3(both)
    for i, c in enumerate(parts):
        if early + i < len(parts):
            fill_jump(traces, nb_ref, bd_ref, jump_ref, face_dofs, elements, parts[early + i])
        values = jnp.concatenate([coef_ref[:, c] * v_ref[:, c], jump_ref[:, c]], axis=0)
        part = rhs[:, c] - dot3(apply3_ref[...], values)
        part_ref[:, c] = part
        ahead_ref[:, c] = dot3(both, part)


def residual_step(
    ahead_ref, v_ref, prev_ref, first_in, second_in, ahead3_ref, coef_ref, nb_ref, bd_ref, send_ref,
    late_ref, dir_ref, end_ref, tr_ref, first_ref, second_ref,
):
    face_dofs = first_in.shape[0]
    dofs, elements = dir_ref.shape
    half = prev_ref.shape[0]
    rim_terms(first_in, second_in, nb_ref, bd_ref, late_ref, face_dofs, elements)
    late_ref[2 * face_dofs :, :] = time_jump_of(v_ref, prev_ref)
    for c in chunks(elements):
        both = (ahead_ref[:, c] - dot3(ahead3_ref[...], late_ref[:, c])) * (1.0 / coef_ref[:, c])
        dir_ref[:, c] = both[:dofs, :]
        end_ref[:, c] = both[half:dofs, :]
        tr_ref[:, c] = both[dofs:, :]
    fill_outbound(tr_ref, send_ref, first_ref, second_ref, face_dofs, elements)


def time_jump_of(v_ref, prev_ref):
    return v_ref[: prev_ref.shape[0], :] - jnp.where(lax.axis_index("tm") > 0, prev_ref[...], 0.0)


def column_sum(x):
    return jnp.sum(x, axis=0, keepdims=True)


def total_sum(row):
    return jnp.sum(row, axis=1, keepdims=True)


def lowest(slope, bend):
    return jnp.where(bend > 0.0, -slope / jnp.where(bend > 0.0, bend, 1.0), 0.0)


def local_second(
    dir_ref, tr_ref, coef_ref, nb_ref, bd_ref, fp3_ref, apply3_ref, late3_ref, part_ref, late_ref, jump0_ref,
    image_ref, border_ref, res_ref, border0_ref, group_ref, traces, jump,
):
    elements = dir_ref.shape[1]
    face_dofs = jump.shape[0] // 6
    rim = 2 * face_dofs
    all_traces(dir_ref, tr_ref, fp3_ref[...], traces)
    for c in chunks(elements):
        fill_jump(traces, nb_ref, bd_ref, jump, face_dofs, elements, c)
        values = jnp.concatenate([coef_ref[:, c] * dir_ref[:, c], jump[:, c]], axis=0)
        image_ref[:, c] = dot3(apply3_ref[...], values)
        res_ref[:, c] = part_ref[:, c] - dot3(late3_ref[...], late_ref[:, c])
        border_ref[:, c] = jump[:rim, c]
        border0_ref[:, c] = jump0_ref[:rim, c] + late_ref[:rim, c]
        j0, j1 = jump0_ref[rim:, c], jump[rim:, c]
        bend, slope = 0.5 * column_sum(j1 * j1), 0.5 * column_sum(j0 * j1)
        best = lowest(slope, bend)
        j = j0 + best * j1
        base = 0.5 * column_sum(j * j)
        group_ref[:, c] = jnp.concatenate([base, slope, bend, best, base, base, base, base], axis=0)


def image_step(
    part_ref, border_ref, dir_ref, prev_ref, first_in, second_in, late3_ref, nb_ref, bd_ref, res_ref, border0_ref, late0_ref, group_ref,
    coeff_ref, sums_ref, late,
):
    face_dofs = first_in.shape[0]
    elements = dir_ref.shape[1]
    rim = 2 * face_dofs
    rim_terms(first_in, second_in, nb_ref, bd_ref, late, face_dofs, elements)
    late[rim:, :] = time_jump_of(dir_ref, prev_ref)
    crosses, squares = [], []
    for c in chunks(elements):
        img = part_ref[:, c] + dot3(late3_ref[...], late[:, c])
        res = res_ref[:, c]
        cross, square = column_sum(res * img), column_sum(img * img)
        j0, j1 = border0_ref[:, c], border_ref[:, c] + late[:rim, c]
        t0, t1 = late0_ref[rim:, c], late[rim:, c]
        g_base, g_slope, g_bend, g_best = (group_ref[i : i + 1, c] for i in range(4))
        bend = square + 0.5 * column_sum(j1 * j1) + column_sum(t1 * t1) + g_bend
        slope = 0.5 * column_sum(j0 * j1) + column_sum(t0 * t1) + g_slope - cross
        best = lowest(slope, bend)
        r = res - best * img
        j = j0 + best * j1
        t = t0 + best * t1
        off = best - g_best
        group = g_base + off * (2.0 * (g_slope + g_best * g_bend) + off * g_bend)
        base = column_sum(r * r) + 0.5 * column_sum(j * j) + column_sum(t * t) + group
        tilt = slope + best * bend
        coeff_ref[:, c] = jnp.concatenate([base, tilt, bend, best, best, best, best, best], axis=0)
        crosses.append(cross)
        squares.append(square)
    base, tilt, bend, best = (coeff_ref[i : i + 1, :] for i in range(4))
    bend_all = total_sum(bend)
    centre = lowest(-total_sum(best * bend), bend_all)
    off = centre - best
    base_all = total_sum(base + off * (2.0 * tilt + off * bend))
    tilt_all = total_sum(tilt + off * bend)
    cross_all = total_sum(jnp.concatenate(crosses, axis=1))
    square_all = total_sum(jnp.concatenate(squares, axis=1))
    lane = lax.broadcasted_iota(jnp.int32, sums_ref.shape, 1)
    out = jnp.zeros(sums_ref.shape, jnp.float32)
    for i, value in enumerate((cross_all, square_all, base_all, tilt_all, bend_all, centre)):
        out = jnp.where(lane == i, value, out)
    sums_ref[...] = out


def last_step(count, all_ref, coeff_ref, v_ref, dir_ref, smooth_ref, ind_ref, est_ref):
    sums = all_ref[...]
    step = jnp.sum(sums[:, 0:1], axis=0, keepdims=True) / jnp.sum(sums[:, 1:2], axis=0, keepdims=True)
    smooth_ref[...] = v_ref[...] + step * dir_ref[...]
    off = step - sums[:, 5:6]
    total = jnp.sum(sums[:, 2:3] + off * (2.0 * sums[:, 3:4] + off * sums[:, 4:5]), axis=0, keepdims=True)
    delta = step - coeff_ref[3:4, :]
    eta = coeff_ref[0:1, :] + delta * (2.0 * coeff_ref[1:2, :] + delta * coeff_ref[2:3, :])
    ind_ref[...] = eta * count / total
    est_ref[...] = jnp.broadcast_to(jnp.sqrt(total / count), est_ref.shape)


VM = pl.BlockSpec(memory_space=pltpu.VMEM)
HB = pl.BlockSpec(memory_space=pltpu.HBM)
F32, BF16 = jnp.float32, jnp.bfloat16


def call(body, name, outs, args, flops, far=(), scratch=()):
    shapes = [jax.ShapeDtypeStruct(*s) if isinstance(s[0], tuple) else jax.ShapeDtypeStruct(s, F32) for s in outs]
    far = tuple(pltpu.with_memory_space_constraint(x, pltpu.HBM) for x in far)
    moved = sum(4 * a.size for a in args + far) + sum(4 * s.size for s in shapes)
    return pl.pallas_call(
        body,
        name=name,
        out_shape=shapes,
        in_specs=[VM] * len(args) + [HB] * len(far),
        out_specs=[VM] * len(outs),
        scratch_shapes=[pltpu.VMEM(s, F32) if isinstance(s, tuple) else s for s in scratch],
        cost_estimate=pl.CostEstimate(flops=flops, bytes_accessed=moved, transcendentals=0),
        compiler_params=pltpu.CompilerParams(vmem_limit_bytes=24 * 2**20),
    )(*args, *far)


def full_swaps(first, slabs, parts):
    other = {i: i + 1 for i in range(first, parts - 1, 2)}
    other.update({j: i for i, j in list(other.items())})
    pairs = []
    for t in range(slabs):
        beside = t ^ 1 if slabs % 2 == 0 else (t + 1) % slabs
        for p in range(parts):
            pairs.append((t * parts + p, t * parts + other[p] if p in other else beside * parts + p))
    return pairs


def on_device(initial, rhs, coef, stiffness, block_inverse, face_proj, lift, time_lift, neighbour, boundary, send_list):
    source = rhs[0]
    dofs, elements = source.shape
    half = time_lift.shape[1]
    traces = face_proj.shape[0]
    face_dofs = traces // 6
    border = send_list.shape[0] // 2
    slabs, parts = lax.axis_size("tm"), lax.axis_size("space")
    devices = slabs * parts
    coef_row = coef.reshape(1, elements)
    send = send_list.reshape(2, border)
    liftt, tlt = lift.T, time_lift.T
    cycle = [(i, (i + 1) % slabs) for i in range(slabs)]

    def halo(a, b):
        swap = lambda x, first: lax.ppermute(x, ("tm", "space"), full_swaps(first, slabs, parts))
        return swap(a, 0), swap(b, 1)

    rim = 2 * face_dofs
    late = rim + half
    edge = (face_dofs, border)
    v0, end0, fp, send, coefs, nb, bd, tr0, a0, b0 = call(
        first_send,
        "send0",
        [(dofs, elements), (half, elements), (traces, dofs), (send.shape, send.dtype), coef_row.shape]
        + [(neighbour.shape, neighbour.dtype), (boundary.shape, boundary.dtype), (rim, elements), edge, edge],
        (),
        2 * rim * dofs * elements,
        far=(initial[0], face_proj, send, coef_row, neighbour, boundary),
        scratch=[pltpu.SemaphoreType.DMA((5 + len(chunks(elements)),))],
    )
    prev0 = lax.ppermute(end0, "tm", cycle)
    a0, b0 = halo(a0, b0)
    jump0, part0, ahead, fp3, apply3, late3, ahead3 = call(
        local_first,
        "local0",
        [(traces, elements), (dofs, elements), (dofs + rim, elements), ((traces - rim, 3 * dofs), BF16)]
        + [((dofs, 3 * (dofs + traces)), BF16), ((dofs, 3 * late), BF16), ((dofs + rim, 3 * late), BF16)],
        (v0, tr0, coefs, fp, nb, bd),
        12 * traces * dofs * elements,
        far=(source, stiffness, block_inverse, liftt, tlt),
        scratch=[(traces, elements), (dofs, elements), (dofs, dofs), (dofs, dofs), (traces, dofs), (half, dofs), pltpu.SemaphoreType.DMA((5,))],
    )
    late0, direction, end, tr1, a1, b1 = call(
        residual_step,
        "residual",
        [(late, elements), (dofs, elements), (half, elements), (rim, elements), edge, edge],
        (ahead, v0, prev0, a0, b0, ahead3, coefs, nb, bd, send),
        6 * dofs * dofs * elements,
    )
    prev1 = lax.ppermute(end, "tm", cycle)
    a1, b1 = halo(a1, b1)
    part1, border1, res, border0, group = call(
        local_second,
        "local1",
        [(dofs, elements), (rim, elements), (dofs, elements), (rim, elements), (SUBS, elements)],
        (direction, tr1, coefs, nb, bd, fp3, apply3, late3, part0, late0, jump0),
        12 * traces * dofs * elements,
        scratch=[(traces, elements), (traces, elements)],
    )
    coeffs, sums = call(
        image_step,
        "image",
        [(SUBS, elements), (devices, LANES)],
        (part1, border1, direction, prev1, a1, b1, late3, nb, bd, res, border0, late0, group),
        6 * dofs * dofs * elements,
        scratch=[(late, elements)],
    )
    everyone = lax.all_to_all(sums, ("tm", "space"), 0, 0, tiled=True)
    smoothed, indicator, estimate = call(
        functools.partial(last_step, float(elements * devices)),
        "last",
        [(dofs, elements), (1, elements), (1, LANES)],
        (everyone, coeffs, v0, direction),
        4 * dofs * elements,
    )
    return smoothed[None], indicator, estimate[0, :1]


def solution(mesh):
    placed = (
        P("tm", None, "space"),
        P("tm", None, "space"),
        P("space"),
        P(),
        P(),
        P(),
        P(),
        P(),
        P(None, "space"),
        P(None, "space"),
        P("space"),
    )
    return jax.shard_map(
        on_device,
        mesh=mesh,
        in_specs=placed,
        out_specs=(P("tm", None, "space"), P("tm", "space"), P()),
        check_vma=False,
    )
```

```python
import functools

import jax
import jax.numpy as jnp
from jax import lax
from jax.experimental import pallas as pl
from jax.experimental.pallas import tpu as pltpu
from jax.sharding import PartitionSpec as P

LANES = 128
SUBS = 8


WIDE = 256


def dot(a, b):
    return jnp.dot(a, b, precision=lax.Precision.HIGHEST, preferred_element_type=jnp.float32)


def split(x):
    high = x.astype(jnp.bfloat16)
    return high, (x - high.astype(jnp.float32)).astype(jnp.bfloat16)


def left3(w):
    high, low = split(w)
    return jnp.concatenate([high, low, high], axis=1)


def dot3(w3, x):
    high, low = split(x)
    return jnp.dot(w3, jnp.concatenate([high, high, low], axis=0), preferred_element_type=jnp.float32)


def chunks(elements):
    width = WIDE if elements % WIDE == 0 else LANES
    return [slice(c, c + width) for c in range(0, elements, width)]


def lane_gather(tile_of, tiles, columns, rows):
    shape = (SUBS, LANES)
    low = jnp.broadcast_to(jnp.bitwise_and(columns, LANES - 1), shape)
    high = jnp.broadcast_to(jnp.right_shift(columns, 7), shape)
    found = [jnp.zeros(shape, jnp.float32) for _ in range(rows // SUBS)]
    for tile in range(tiles):
        here = high == tile
        for r in range(rows // SUBS):
            picked = jnp.take_along_axis(tile_of(tile, r), low, axis=1)
            found[r] = jnp.where(here, picked, found[r])
    return found


def face_rows(ref, face, face_dofs):
    return ref[pl.ds(face, face_dofs, stride=6), :]


def is_odd():
    return lax.rem(lax.axis_index("space"), 2) == 1


def fill_outbound(traces, send_ref, first_ref, second_ref, face_dofs, elements):
    per_face = elements // LANES
    odd = is_odd()

    def tile_of(tile, r):
        face, col = divmod(tile, per_face)
        return traces[face * face_dofs + r * SUBS : face * face_dofs + (r + 1) * SUBS, col * LANES : (col + 1) * LANES]

    border = send_ref.shape[1]
    for j in range(border // LANES):
        cols = slice(j * LANES, (j + 1) * LANES)
        lower = lane_gather(tile_of, 2 * per_face, send_ref[0:1, cols], face_dofs)
        upper = lane_gather(tile_of, 2 * per_face, send_ref[1:2, cols], face_dofs)
        for r in range(face_dofs // SUBS):
            rows = slice(r * SUBS, (r + 1) * SUBS)
            first_ref[rows, cols] = jnp.where(odd, lower[r], upper[r])
            second_ref[rows, cols] = jnp.where(odd, upper[r], lower[r])


def fill_jump(traces, nb_ref, bd_ref, jump_ref, face_dofs, elements, chunk):
    per_face = elements // LANES
    for face in range(6):
        other = face ^ 1

        def tile_of(tile, r, other=other):
            return traces[other * face_dofs + r * SUBS : other * face_dofs + (r + 1) * SUBS, tile * LANES : (tile + 1) * LANES]

        for start in range(chunk.start, chunk.stop, LANES):
            cols = slice(start, start + LANES)
            found = lane_gather(tile_of, per_face, nb_ref[face : face + 1, cols] - other * elements, face_dofs)
            open_face = jnp.broadcast_to(1.0 - bd_ref[face : face + 1, cols].astype(jnp.float32), (SUBS, LANES))
            for r in range(face_dofs // SUBS):
                rows = slice(face * face_dofs + r * SUBS, face * face_dofs + (r + 1) * SUBS)
                jump_ref[rows, cols] = traces[rows, cols] - found[r] * open_face


def rim_terms(first_ref, second_ref, nb_ref, bd_ref, rim_ref, face_dofs, elements):
    tiles = first_ref.shape[1] // LANES
    odd, place, parts = is_odd(), lax.axis_index("space"), lax.axis_size("space")
    sides = []
    for side in range(2):
        for t in range(tiles):
            cols = slice(t * LANES, (t + 1) * LANES)
            a, b = first_ref[:, cols], second_ref[:, cols]
            values = jnp.where(odd, a, b) if side == 0 else jnp.where(odd, b, a)
            there = place > 0 if side == 0 else place < parts - 1
            sides.append(jnp.where(there, values, 0.0))

    def tile_of(tile, r):
        return sides[tile][r * SUBS : (r + 1) * SUBS, :]

    for j in range(elements // LANES):
        cols = slice(j * LANES, (j + 1) * LANES)
        for face in range(2):
            found = lane_gather(tile_of, 2 * tiles, nb_ref[face : face + 1, cols] - 6 * elements, face_dofs)
            open_face = jnp.broadcast_to(1.0 - bd_ref[face : face + 1, cols].astype(jnp.float32), (SUBS, LANES))
            for r in range(face_dofs // SUBS):
                rows = slice(face * face_dofs + r * SUBS, face * face_dofs + (r + 1) * SUBS)
                rim_ref[rows, cols] = 0.0 - found[r] * open_face


def load_first(
    v_hbm, fp_hbm, send_hbm, coef_hbm, nb_hbm, bd_hbm, v_ref, end_ref, fp_ref, send_ref, coef_ref, nb_ref, bd_ref, sems
):
    half = end_ref.shape[0]
    pairs = ((v_hbm, v_ref), (fp_hbm, fp_ref), (send_hbm, send_ref), (coef_hbm, coef_ref), (nb_hbm, nb_ref), (bd_hbm, bd_ref))
    copies = [pltpu.make_async_copy(a, b, sems.at[i]) for i, (a, b) in enumerate(pairs)]
    for copy in copies:
        copy.start()
    copies[0].wait()
    end_ref[...] = v_ref[half:, :]
    for copy in copies[1:]:
        copy.wait()


def first_send(v_ref, fp_ref, send_ref, tr_ref, first_ref, second_ref):
    face_dofs = fp_ref.shape[0] // 6
    elements = v_ref.shape[1]
    weights = left3(jnp.concatenate([face_rows(fp_ref, f, face_dofs) for f in range(2)], axis=0))
    for c in chunks(elements):
        tr_ref[:, c] = dot3(weights, v_ref[:, c])
    fill_outbound(tr_ref, send_ref, first_ref, second_ref, face_dofs, elements)


def all_traces(v_ref, tr_ref, weights, traces):
    known = tr_ref.shape[0]
    for c in chunks(v_ref.shape[1]):
        traces[:known, c] = tr_ref[:, c]
        traces[known:, c] = dot3(weights, v_ref[:, c])


def local_first(
    v_ref, tr_ref, coef_ref, fp_ref, nb_ref, bd_ref, rhs_hbm, stiff_hbm, inv_hbm, liftt_hbm, tlt_hbm,
    jump_ref, part_ref, ahead_ref, fp3_ref, apply3_ref, late3_ref, ahead3_ref,
    traces, rhs, stiff, inv, liftt, tlt, sems,
):
    face_dofs = fp_ref.shape[0] // 6
    elements = v_ref.shape[1]
    pairs = ((stiff_hbm, stiff), (liftt_hbm, liftt), (tlt_hbm, tlt), (inv_hbm, inv), (rhs_hbm, rhs))
    copies = [pltpu.make_async_copy(a, b, sems.at[i]) for i, (a, b) in enumerate(pairs)]
    for copy in copies:
        copy.start()
    fp3_ref[...] = left3(jnp.concatenate([face_rows(fp_ref, f, face_dofs) for f in range(2, 6)], axis=0))
    all_traces(v_ref, tr_ref, fp3_ref[...], traces)
    parts = chunks(elements)
    early = (len(parts) + 1) // 2
    for c in parts[:early]:
        fill_jump(traces, nb_ref, bd_ref, jump_ref, face_dofs, elements, c)
    for copy in copies[:4]:
        copy.wait()
    lift_rows = [face_rows(liftt, f, face_dofs) for f in range(6)]
    apply3_ref[...] = left3(jnp.concatenate([stiff[...], jnp.concatenate(lift_rows, axis=0).T], axis=1))
    late = jnp.concatenate(lift_rows[:2] + [tlt[...]], axis=0).T
    late3_ref[...] = left3(late)
    inverse = inv[...]
    first_faces = jnp.concatenate([face_rows(fp_ref, f, face_dofs) for f in range(2)], axis=0)
    both = jnp.concatenate([inverse, dot(first_faces, inverse)], axis=0)
    ahead3_ref[...] = left3(dot(both, late))
    both = left3(both)
    def apply(c):
        values = jnp.concatenate([coef_ref[:, c] * v_ref[:, c], jump_ref[:, c]], axis=0)
        part_ref[:, c] = dot3(apply3_ref[...], values)

    def subtract(c):
        part = rhs[:, c] - part_ref[:, c]
        part_ref[:, c] = part
        ahead_ref[:, c] = dot3(both, part)

    for i, c in enumerate(parts[early:]):
        apply(parts[i])
        if i == len(parts) - early - 1:
            copies[4].wait()
        fill_jump(traces, nb_ref, bd_ref, jump_ref, face_dofs, elements, c)
    for i in range(len(parts)):
        if len(parts) - early + i < len(parts):
            apply(parts[len(parts) - early + i])
        subtract(parts[i])


def end_step(ahead_ref, v_ref, prev_ref, first_in, second_in, ahead3_ref, coef_ref, nb_ref, bd_ref, late_ref, end_ref):
    face_dofs = first_in.shape[0]
    elements = v_ref.shape[1]
    half = prev_ref.shape[0]
    dofs = v_ref.shape[0]
    rim_terms(first_in, second_in, nb_ref, bd_ref, late_ref, face_dofs, elements)
    late_ref[2 * face_dofs :, :] = time_jump_of(v_ref, prev_ref)
    for c in chunks(elements):
        end_ref[:, c] = (ahead_ref[half:dofs, c] - dot3(ahead3_ref[half:dofs, :], late_ref[:, c])) * (1.0 / coef_ref[:, c])


def rest_step(ahead_ref, late_ref, end_ref, ahead3_ref, coef_ref, send_ref, dir_ref, tr_ref, first_ref, second_ref):
    face_dofs = first_ref.shape[0]
    dofs, elements = dir_ref.shape
    half = end_ref.shape[0]
    weights = jnp.concatenate([ahead3_ref[dofs:, :], ahead3_ref[:half, :]], axis=0)
    rim = 2 * face_dofs
    for c in chunks(elements):
        scale = 1.0 / coef_ref[:, c]
        both = dot3(weights, late_ref[:, c])
        tr_ref[:, c] = (ahead_ref[dofs:, c] - both[:rim, :]) * scale
        dir_ref[:half, c] = (ahead_ref[:half, c] - both[rim:, :]) * scale
        dir_ref[half:, c] = end_ref[:, c]
    fill_outbound(tr_ref, send_ref, first_ref, second_ref, face_dofs, elements)


def time_jump_of(v_ref, prev_ref):
    return v_ref[: prev_ref.shape[0], :] - jnp.where(lax.axis_index("tm") > 0, prev_ref[...], 0.0)


def column_sum(x):
    return jnp.sum(x, axis=0, keepdims=True)


def total_sum(row):
    return jnp.sum(row, axis=1, keepdims=True)


def lowest(slope, bend):
    return jnp.where(bend > 0.0, -slope / jnp.where(bend > 0.0, bend, 1.0), 0.0)


def local_second(
    dir_ref, tr_ref, coef_ref, nb_ref, bd_ref, fp3_ref, apply3_ref, late3_ref, part_ref, late_ref, jump0_ref,
    image_ref, border_ref, res_ref, border0_ref, group_ref, traces, jump,
):
    elements = dir_ref.shape[1]
    face_dofs = jump.shape[0] // 6
    rim = 2 * face_dofs
    all_traces(dir_ref, tr_ref, fp3_ref[...], traces)
    for c in chunks(elements):
        fill_jump(traces, nb_ref, bd_ref, jump, face_dofs, elements, c)
        values = jnp.concatenate([coef_ref[:, c] * dir_ref[:, c], jump[:, c]], axis=0)
        image_ref[:, c] = dot3(apply3_ref[...], values)
        res_ref[:, c] = part_ref[:, c] - dot3(late3_ref[...], late_ref[:, c])
        border_ref[:, c] = jump[:rim, c]
        border0_ref[:, c] = jump0_ref[:rim, c] + late_ref[:rim, c]
        j0, j1 = jump0_ref[rim:, c], jump[rim:, c]
        bend, slope = 0.5 * column_sum(j1 * j1), 0.5 * column_sum(j0 * j1)
        best = lowest(slope, bend)
        j = j0 + best * j1
        base = 0.5 * column_sum(j * j)
        group_ref[:, c] = jnp.concatenate([base, slope, bend, best, base, base, base, base], axis=0)


def image_step(
    part_ref, border_ref, dir_ref, prev_ref, first_in, second_in, late3_ref, nb_ref, bd_ref, res_ref, border0_ref, late0_ref, group_ref,
    coeff_ref, sums_ref, late,
):
    face_dofs = first_in.shape[0]
    elements = dir_ref.shape[1]
    rim = 2 * face_dofs
    rim_terms(first_in, second_in, nb_ref, bd_ref, late, face_dofs, elements)
    late[rim:, :] = time_jump_of(dir_ref, prev_ref)
    crosses, squares = [], []
    for c in chunks(elements):
        img = part_ref[:, c] + dot3(late3_ref[...], late[:, c])
        res = res_ref[:, c]
        cross, square = column_sum(res * img), column_sum(img * img)
        j0, j1 = border0_ref[:, c], border_ref[:, c] + late[:rim, c]
        t0, t1 = late0_ref[rim:, c], late[rim:, c]
        g_base, g_slope, g_bend, g_best = (group_ref[i : i + 1, c] for i in range(4))
        bend = square + 0.5 * column_sum(j1 * j1) + column_sum(t1 * t1) + g_bend
        slope = 0.5 * column_sum(j0 * j1) + column_sum(t0 * t1) + g_slope - cross
        best = lowest(slope, bend)
        r = res - best * img
        j = j0 + best * j1
        t = t0 + best * t1
        off = best - g_best
        group = g_base + off * (2.0 * (g_slope + g_best * g_bend) + off * g_bend)
        base = column_sum(r * r) + 0.5 * column_sum(j * j) + column_sum(t * t) + group
        tilt = slope + best * bend
        coeff_ref[:, c] = jnp.concatenate([base, tilt, bend, best, best, best, best, best], axis=0)
        crosses.append(cross)
        squares.append(square)
    base, tilt, bend, best = (coeff_ref[i : i + 1, :] for i in range(4))
    bend_all = total_sum(bend)
    centre = lowest(-total_sum(best * bend), bend_all)
    off = centre - best
    base_all = total_sum(base + off * (2.0 * tilt + off * bend))
    tilt_all = total_sum(tilt + off * bend)
    cross_all = total_sum(jnp.concatenate(crosses, axis=1))
    square_all = total_sum(jnp.concatenate(squares, axis=1))
    lane = lax.broadcasted_iota(jnp.int32, sums_ref.shape, 1)
    out = jnp.zeros(sums_ref.shape, jnp.float32)
    for i, value in enumerate((cross_all, square_all, base_all, tilt_all, bend_all, centre)):
        out = jnp.where(lane == i, value, out)
    sums_ref[...] = out


def last_step(count, all_ref, coeff_ref, v_ref, dir_ref, smooth_ref, ind_ref, est_ref):
    sums = all_ref[...]
    step = jnp.sum(sums[:, 0:1], axis=0, keepdims=True) / jnp.sum(sums[:, 1:2], axis=0, keepdims=True)
    smooth_ref[...] = v_ref[...] + step * dir_ref[...]
    off = step - sums[:, 5:6]
    total = jnp.sum(sums[:, 2:3] + off * (2.0 * sums[:, 3:4] + off * sums[:, 4:5]), axis=0, keepdims=True)
    delta = step - coeff_ref[3:4, :]
    eta = coeff_ref[0:1, :] + delta * (2.0 * coeff_ref[1:2, :] + delta * coeff_ref[2:3, :])
    ind_ref[...] = eta * count / total
    est_ref[...] = jnp.broadcast_to(jnp.sqrt(total / count), est_ref.shape)


VM = pl.BlockSpec(memory_space=pltpu.VMEM)
HB = pl.BlockSpec(memory_space=pltpu.HBM)
F32, BF16 = jnp.float32, jnp.bfloat16


def call(body, name, outs, args, flops, far=(), scratch=()):
    shapes = [jax.ShapeDtypeStruct(*s) if isinstance(s[0], tuple) else jax.ShapeDtypeStruct(s, F32) for s in outs]
    far = tuple(pltpu.with_memory_space_constraint(x, pltpu.HBM) for x in far)
    moved = sum(4 * a.size for a in args + far) + sum(4 * s.size for s in shapes)
    return pl.pallas_call(
        body,
        name=name,
        out_shape=shapes,
        in_specs=[VM] * len(args) + [HB] * len(far),
        out_specs=[VM] * len(outs),
        scratch_shapes=[pltpu.VMEM(s, F32) if isinstance(s, tuple) else s for s in scratch],
        cost_estimate=pl.CostEstimate(flops=flops, bytes_accessed=moved, transcendentals=0),
        compiler_params=pltpu.CompilerParams(vmem_limit_bytes=24 * 2**20),
    )(*args, *far)


def full_swaps(first, slabs, parts):
    other = {i: i + 1 for i in range(first, parts - 1, 2)}
    other.update({j: i for i, j in list(other.items())})
    pairs = []
    for t in range(slabs):
        beside = t ^ 1 if slabs % 2 == 0 else (t + 1) % slabs
        for p in range(parts):
            pairs.append((t * parts + p, t * parts + other[p] if p in other else beside * parts + p))
    return pairs


def on_device(initial, rhs, coef, stiffness, block_inverse, face_proj, lift, time_lift, neighbour, boundary, send_list):
    source = rhs[0]
    dofs, elements = source.shape
    half = time_lift.shape[1]
    traces = face_proj.shape[0]
    face_dofs = traces // 6
    border = send_list.shape[0] // 2
    slabs, parts = lax.axis_size("tm"), lax.axis_size("space")
    devices = slabs * parts
    coef_row = coef.reshape(1, elements)
    send = send_list.reshape(2, border)
    liftt, tlt = lift.T, time_lift.T
    cycle = [(i, (i + 1) % slabs) for i in range(slabs)]

    def halo(a, b):
        swap = lambda x, first: lax.ppermute(x, ("tm", "space"), full_swaps(first, slabs, parts))
        return swap(a, 0), swap(b, 1)

    rim = 2 * face_dofs
    late = rim + half
    edge = (face_dofs, border)
    v0, end0, fp, send, coefs, nb, bd = call(
        load_first,
        "load",
        [(dofs, elements), (half, elements), (traces, dofs), (send.shape, send.dtype), coef_row.shape]
        + [(neighbour.shape, neighbour.dtype), (boundary.shape, boundary.dtype)],
        (),
        0,
        far=(initial[0], face_proj, send, coef_row, neighbour, boundary),
        scratch=[pltpu.SemaphoreType.DMA((6,))],
    )
    prev0 = lax.ppermute(end0, "tm", cycle)
    tr0, a0, b0 = call(first_send, "send0", [(rim, elements), edge, edge], (v0, fp, send), 2 * rim * dofs * elements)
    a0, b0 = halo(a0, b0)
    jump0, part0, ahead, fp3, apply3, late3, ahead3 = call(
        local_first,
        "local0",
        [(traces, elements), (dofs, elements), (dofs + rim, elements), ((traces - rim, 3 * dofs), BF16)]
        + [((dofs, 3 * (dofs + traces)), BF16), ((dofs, 3 * late), BF16), ((dofs + rim, 3 * late), BF16)],
        (v0, tr0, coefs, fp, nb, bd),
        12 * traces * dofs * elements,
        far=(source, stiffness, block_inverse, liftt, tlt),
        scratch=[(traces, elements), (dofs, elements), (dofs, dofs), (dofs, dofs), (traces, dofs), (half, dofs), pltpu.SemaphoreType.DMA((5,))],
    )
    late0, end = call(
        end_step,
        "end",
        [(late, elements), (half, elements)],
        (ahead, v0, prev0, a0, b0, ahead3, coefs, nb, bd),
        6 * half * dofs * elements,
    )
    prev1 = lax.ppermute(end, "tm", cycle)
    direction, tr1, a1, b1 = call(
        rest_step,
        "rest",
        [(dofs, elements), (rim, elements), edge, edge],
        (ahead, late0, end, ahead3, coefs, send),
        6 * dofs * dofs * elements,
    )
    a1, b1 = halo(a1, b1)
    part1, border1, res, border0, group = call(
        local_second,
        "local1",
        [(dofs, elements), (rim, elements), (dofs, elements), (rim, elements), (SUBS, elements)],
        (direction, tr1, coefs, nb, bd, fp3, apply3, late3, part0, late0, jump0),
        12 * traces * dofs * elements,
        scratch=[(traces, elements), (traces, elements)],
    )
    coeffs, sums = call(
        image_step,
        "image",
        [(SUBS, elements), (devices, LANES)],
        (part1, border1, direction, prev1, a1, b1, late3, nb, bd, res, border0, late0, group),
        6 * dofs * dofs * elements,
        scratch=[(late, elements)],
    )
    everyone = lax.all_to_all(sums, ("tm", "space"), 0, 0, tiled=True)
    smoothed, indicator, estimate = call(
        functools.partial(last_step, float(elements * devices)),
        "last",
        [(dofs, elements), (1, elements), (1, LANES)],
        (everyone, coeffs, v0, direction),
        4 * dofs * elements,
    )
    return smoothed[None], indicator, estimate[0, :1]


def solution(mesh):
    placed = (
        P("tm", None, "space"),
        P("tm", None, "space"),
        P("space"),
        P(),
        P(),
        P(),
        P(),
        P(),
        P(None, "space"),
        P(None, "space"),
        P("space"),
    )
    return jax.shard_map(
        on_device,
        mesh=mesh,
        in_specs=placed,
        out_specs=(P("tm", None, "space"), P("tm", "space"), P()),
        check_vma=False,
    )
```

```python
import functools

import jax
import jax.numpy as jnp
from jax import lax
from jax.experimental import pallas as pl
from jax.experimental.pallas import tpu as pltpu
from jax.sharding import PartitionSpec as P

LANES = 128
SUBS = 8


WIDE = 512
SELECTED = (2, 3)


def dot(a, b):
    return jnp.dot(a, b, precision=lax.Precision.HIGHEST, preferred_element_type=jnp.float32)


def split(x):
    high = x.astype(jnp.bfloat16)
    return high, (x - high.astype(jnp.float32)).astype(jnp.bfloat16)


def left3(w):
    high, low = split(w)
    return jnp.concatenate([high, low, high], axis=1)


def dot3(w3, x):
    high, low = split(x)
    return jnp.dot(w3, jnp.concatenate([high, high, low], axis=0), preferred_element_type=jnp.float32)


def chunks(elements):
    width = WIDE if elements % WIDE == 0 else LANES
    return [slice(c, c + width) for c in range(0, elements, width)]


def lane_gather(tile_of, tiles, columns, rows):
    shape = (SUBS, LANES)
    low = jnp.broadcast_to(jnp.bitwise_and(columns, LANES - 1), shape)
    high = jnp.broadcast_to(jnp.right_shift(columns, 7), shape)
    found = [jnp.zeros(shape, jnp.float32) for _ in range(rows // SUBS)]
    for tile in range(tiles):
        here = high == tile
        for r in range(rows // SUBS):
            picked = jnp.take_along_axis(tile_of(tile, r), low, axis=1)
            found[r] = jnp.where(here, picked, found[r])
    return found


def face_rows(ref, face, face_dofs):
    return ref[pl.ds(face, face_dofs, stride=6), :]


def is_odd():
    return lax.rem(lax.axis_index("space"), 2) == 1


def fill_outbound(traces, send_ref, first_ref, second_ref, face_dofs, elements):
    per_face = elements // LANES
    odd = is_odd()

    def tile_of(tile, r):
        face, col = divmod(tile, per_face)
        return traces[face * face_dofs + r * SUBS : face * face_dofs + (r + 1) * SUBS, col * LANES : (col + 1) * LANES]

    border = send_ref.shape[1]
    for j in range(border // LANES):
        cols = slice(j * LANES, (j + 1) * LANES)
        lower = lane_gather(tile_of, 2 * per_face, send_ref[0:1, cols], face_dofs)
        upper = lane_gather(tile_of, 2 * per_face, send_ref[1:2, cols], face_dofs)
        for r in range(face_dofs // SUBS):
            rows = slice(r * SUBS, (r + 1) * SUBS)
            first_ref[rows, cols] = jnp.where(odd, lower[r], upper[r])
            second_ref[rows, cols] = jnp.where(odd, upper[r], lower[r])


def thirds(x):
    high = x.astype(jnp.bfloat16)
    rest = x - high.astype(jnp.float32)
    middle = rest.astype(jnp.bfloat16)
    return jnp.concatenate([high, middle, (rest - middle.astype(jnp.float32)).astype(jnp.bfloat16)], axis=0)


def fill_jump(traces, terms, nb_ref, bd_ref, jump_ref, face_dofs, elements, chunk):
    per_face = elements // LANES
    width = chunk.stop - chunk.start
    for face in range(6):
        other = face ^ 1
        if face in SELECTED:
            columns = nb_ref[face : face + 1, chunk] - other * elements
            block = 2 * LANES if elements % (2 * LANES) == 0 else LANES
            number = lax.broadcasted_iota(jnp.int32, (block, width), 0).astype(jnp.float32).astype(jnp.bfloat16)
            picks = []
            for start in range(0, elements, block):
                place = jnp.clip(columns - start, -1, block).astype(jnp.float32).astype(jnp.bfloat16)
                picks.append(jnp.where(number == jnp.broadcast_to(place, (block, width)), jnp.bfloat16(1), jnp.bfloat16(0)))
            at = SELECTED.index(other) * 3 * face_dofs
            found = jnp.dot(terms[at : at + 3 * face_dofs, :], jnp.concatenate(picks, axis=0), preferred_element_type=jnp.float32)
            found = (found[:face_dofs] + found[face_dofs : 2 * face_dofs]) + found[2 * face_dofs :]
            rows = slice(face * face_dofs, (face + 1) * face_dofs)
            jump_ref[rows, chunk] = traces[rows, chunk] - found * (1.0 - bd_ref[face : face + 1, chunk].astype(jnp.float32))
            continue

        def tile_of(tile, r, other=other):
            return traces[other * face_dofs + r * SUBS : other * face_dofs + (r + 1) * SUBS, tile * LANES : (tile + 1) * LANES]

        for start in range(chunk.start, chunk.stop, LANES):
            cols = slice(start, start + LANES)
            found = lane_gather(tile_of, per_face, nb_ref[face : face + 1, cols] - other * elements, face_dofs)
            open_face = jnp.broadcast_to(1.0 - bd_ref[face : face + 1, cols].astype(jnp.float32), (SUBS, LANES))
            for r in range(face_dofs // SUBS):
                rows = slice(face * face_dofs + r * SUBS, face * face_dofs + (r + 1) * SUBS)
                jump_ref[rows, cols] = traces[rows, cols] - found[r] * open_face


def rim_terms(first_ref, second_ref, nb_ref, bd_ref, rim_ref, face_dofs, elements):
    tiles = first_ref.shape[1] // LANES
    odd, place, parts = is_odd(), lax.axis_index("space"), lax.axis_size("space")
    sides = []
    for side in range(2):
        for t in range(tiles):
            cols = slice(t * LANES, (t + 1) * LANES)
            a, b = first_ref[:, cols], second_ref[:, cols]
            values = jnp.where(odd, a, b) if side == 0 else jnp.where(odd, b, a)
            there = place > 0 if side == 0 else place < parts - 1
            sides.append(jnp.where(there, values, 0.0))

    def tile_of(tile, r):
        return sides[tile][r * SUBS : (r + 1) * SUBS, :]

    for j in range(elements // LANES):
        cols = slice(j * LANES, (j + 1) * LANES)
        for face in range(2):
            found = lane_gather(tile_of, 2 * tiles, nb_ref[face : face + 1, cols] - 6 * elements, face_dofs)
            open_face = jnp.broadcast_to(1.0 - bd_ref[face : face + 1, cols].astype(jnp.float32), (SUBS, LANES))
            for r in range(face_dofs // SUBS):
                rows = slice(face * face_dofs + r * SUBS, face * face_dofs + (r + 1) * SUBS)
                rim_ref[rows, cols] = 0.0 - found[r] * open_face


def load_first(
    v_hbm, fp_hbm, send_hbm, coef_hbm, nb_hbm, bd_hbm, v_ref, end_ref, fp_ref, send_ref, coef_ref, nb_ref, bd_ref, sems
):
    half = end_ref.shape[0]
    pairs = ((v_hbm, v_ref), (fp_hbm, fp_ref), (send_hbm, send_ref), (coef_hbm, coef_ref), (nb_hbm, nb_ref), (bd_hbm, bd_ref))
    copies = [pltpu.make_async_copy(a, b, sems.at[i]) for i, (a, b) in enumerate(pairs)]
    for copy in copies:
        copy.start()
    copies[0].wait()
    end_ref[...] = v_ref[half:, :]
    for copy in copies[1:]:
        copy.wait()


def first_send(v_ref, fp_ref, send_ref, tr_ref, first_ref, second_ref):
    face_dofs = fp_ref.shape[0] // 6
    elements = v_ref.shape[1]
    weights = left3(jnp.concatenate([face_rows(fp_ref, f, face_dofs) for f in range(2)], axis=0))
    for c in chunks(elements):
        tr_ref[:, c] = dot3(weights, v_ref[:, c])
    fill_outbound(tr_ref, send_ref, first_ref, second_ref, face_dofs, elements)


def all_traces(v_ref, tr_ref, weights, traces, terms):
    known = tr_ref.shape[0]
    face_dofs = traces.shape[0] // 6
    for c in chunks(v_ref.shape[1]):
        traces[:known, c] = tr_ref[:, c]
        traces[known:, c] = dot3(weights, v_ref[:, c])
        for i, face in enumerate(SELECTED):
            terms[3 * i * face_dofs : 3 * (i + 1) * face_dofs, c] = thirds(traces[face * face_dofs : (face + 1) * face_dofs, c])


def local_first(
    v_ref, tr_ref, coef_ref, fp_ref, nb_ref, bd_ref, stiff, inv, liftt, tlt, rhs,
    jump_ref, part_ref, ahead_ref, fp3_ref, apply3_ref, rim3_ref, time3_ref, ahead_rim3_ref, ahead_time3_ref,
    traces, terms,
):
    face_dofs = fp_ref.shape[0] // 6
    elements = v_ref.shape[1]
    fp3_ref[...] = left3(jnp.concatenate([face_rows(fp_ref, f, face_dofs) for f in range(2, 6)], axis=0))
    all_traces(v_ref, tr_ref, fp3_ref[...], traces, terms)
    lift_rows = [face_rows(liftt, f, face_dofs) for f in range(6)]
    apply3_ref[...] = left3(jnp.concatenate([stiff[...], jnp.concatenate(lift_rows, axis=0).T], axis=1))
    rim, time = jnp.concatenate(lift_rows[:2], axis=0).T, tlt[...].T
    rim3_ref[...] = left3(rim)
    time3_ref[...] = left3(time)
    inverse = inv[...]
    first_faces = jnp.concatenate([face_rows(fp_ref, f, face_dofs) for f in range(2)], axis=0)
    both = jnp.concatenate([inverse, dot(first_faces, inverse)], axis=0)
    ahead_rim3_ref[...] = left3(dot(both, rim))
    ahead_time3_ref[...] = left3(dot(both, time))
    both = left3(both)
    for c in chunks(elements):
        fill_jump(traces, terms, nb_ref, bd_ref, jump_ref, face_dofs, elements, c)
        values = jnp.concatenate([coef_ref[:, c] * v_ref[:, c], jump_ref[:, c]], axis=0)
        part = rhs[:, c] - dot3(apply3_ref[...], values)
        part_ref[:, c] = part
        ahead_ref[:, c] = dot3(both, part)


def edge_first(ahead_ref, first_in, second_in, ahead_rim3_ref, nb_ref, bd_ref, near_ref, rim_ref):
    rim_terms(first_in, second_in, nb_ref, bd_ref, rim_ref, first_in.shape[0], near_ref.shape[1])
    for c in chunks(near_ref.shape[1]):
        near_ref[:, c] = ahead_ref[:, c] - dot3(ahead_rim3_ref[...], rim_ref[:, c])


def end_step(near_ref, v_ref, prev_ref, ahead_time3_ref, coef_ref, time_ref, end_ref):
    dofs, elements = v_ref.shape
    half = prev_ref.shape[0]
    time_ref[...] = time_jump_of(v_ref, prev_ref)
    for c in chunks(elements):
        end_ref[:, c] = (near_ref[half:dofs, c] - dot3(ahead_time3_ref[half:dofs, :], time_ref[:, c])) * (1.0 / coef_ref[:, c])


def rest_step(near_ref, time_ref, end_ref, ahead_time3_ref, coef_ref, send_ref, dir_ref, tr_ref, first_ref, second_ref):
    face_dofs = first_ref.shape[0]
    dofs, elements = dir_ref.shape
    half = end_ref.shape[0]
    weights = jnp.concatenate([ahead_time3_ref[dofs:, :], ahead_time3_ref[:half, :]], axis=0)
    rim = 2 * face_dofs
    for c in chunks(elements):
        scale = 1.0 / coef_ref[:, c]
        both = dot3(weights, time_ref[:, c])
        tr_ref[:, c] = (near_ref[dofs:, c] - both[:rim, :]) * scale
        dir_ref[:half, c] = (near_ref[:half, c] - both[rim:, :]) * scale
        dir_ref[half:, c] = end_ref[:, c]
    fill_outbound(tr_ref, send_ref, first_ref, second_ref, face_dofs, elements)


def time_jump_of(v_ref, prev_ref):
    return v_ref[: prev_ref.shape[0], :] - jnp.where(lax.axis_index("tm") > 0, prev_ref[...], 0.0)


def column_sum(x):
    return jnp.sum(x, axis=0, keepdims=True)


def total_sum(row):
    return jnp.sum(row, axis=1, keepdims=True)


def lowest(slope, bend):
    return jnp.where(bend > 0.0, -slope / jnp.where(bend > 0.0, bend, 1.0), 0.0)


def group_sums(j0, j1):
    bend, slope = 0.5 * column_sum(j1 * j1), 0.5 * column_sum(j0 * j1)
    best = lowest(slope, bend)
    j = j0 + best * j1
    return [0.5 * column_sum(j * j), slope, bend, best]


def group_at(group, s):
    base, slope, bend, best = group
    off = s - best
    return base + off * (2.0 * (slope + best * bend) + off * bend)


def local_second(
    dir_ref, tr_ref, coef_ref, nb_ref, bd_ref, fp3_ref, apply3_ref, rim3_ref, time3_ref, part_ref, rim_ref, time_ref, jump0_ref,
    image_ref, border_ref, res_ref, border0_ref, group_ref, traces, terms, jump,
):
    elements = dir_ref.shape[1]
    face_dofs = jump.shape[0] // 6
    rim = 2 * face_dofs
    all_traces(dir_ref, tr_ref, fp3_ref[...], traces, terms)
    for c in chunks(elements):
        fill_jump(traces, terms, nb_ref, bd_ref, jump, face_dofs, elements, c)
        values = jnp.concatenate([coef_ref[:, c] * dir_ref[:, c], jump[:, c]], axis=0)
        image_ref[:, c] = dot3(apply3_ref[...], values)
        res_ref[:, c] = part_ref[:, c] - dot3(rim3_ref[...], rim_ref[:, c]) - dot3(time3_ref[...], time_ref[:, c])
        border_ref[:, c] = jump[:rim, c]
        border0_ref[:, c] = jump0_ref[:rim, c] + rim_ref[:, c]
        group_ref[:, c] = jnp.concatenate(group_sums(jump0_ref[rim:, c], jump[rim:, c]) * 2, axis=0)


def edge_second(part_ref, border_ref, first_in, second_in, rim3_ref, nb_ref, bd_ref, border0_ref, group_ref, near_ref, groups_ref, rim):
    elements = part_ref.shape[1]
    rim_terms(first_in, second_in, nb_ref, bd_ref, rim, first_in.shape[0], elements)
    for c in chunks(elements):
        near_ref[:, c] = part_ref[:, c] + dot3(rim3_ref[...], rim[:, c])
        sums = group_sums(border0_ref[:, c], border_ref[:, c] + rim[:, c])
        groups_ref[:, c] = jnp.concatenate([group_ref[:4, c]] + sums, axis=0)


def image_step(near_ref, dir_ref, prev_ref, time3_ref, res_ref, time0_ref, group_ref, coeff_ref, sums_ref, time):
    elements = dir_ref.shape[1]
    crosses, squares = [], []
    time[...] = time_jump_of(dir_ref, prev_ref)
    for c in chunks(elements):
        t0, t1 = time0_ref[:, c], time[:, c]
        img = near_ref[:, c] + dot3(time3_ref[...], t1)
        res = res_ref[:, c]
        cross, square = column_sum(res * img), column_sum(img * img)
        groups = [[group_ref[i : i + 1, c] for i in range(k, k + 4)] for k in (0, 4)]
        bend = square + column_sum(t1 * t1) + groups[0][2] + groups[1][2]
        slope = column_sum(t0 * t1) + groups[0][1] + groups[1][1] - cross
        best = lowest(slope, bend)
        r = res - best * img
        t = t0 + best * t1
        base = column_sum(r * r) + column_sum(t * t) + group_at(groups[0], best) + group_at(groups[1], best)
        tilt = slope + best * bend
        coeff_ref[:, c] = jnp.concatenate([base, tilt, bend, best, best, best, best, best], axis=0)
        crosses.append(cross)
        squares.append(square)
    base, tilt, bend, best = (coeff_ref[i : i + 1, :] for i in range(4))
    bend_all = total_sum(bend)
    centre = lowest(-total_sum(best * bend), bend_all)
    off = centre - best
    base_all = total_sum(base + off * (2.0 * tilt + off * bend))
    tilt_all = total_sum(tilt + off * bend)
    cross_all = total_sum(jnp.concatenate(crosses, axis=1))
    square_all = total_sum(jnp.concatenate(squares, axis=1))
    lane = lax.broadcasted_iota(jnp.int32, sums_ref.shape, 1)
    out = jnp.zeros(sums_ref.shape, jnp.float32)
    for i, value in enumerate((cross_all, square_all, base_all, tilt_all, bend_all, centre)):
        out = jnp.where(lane == i, value, out)
    sums_ref[...] = out


def last_step(count, all_ref, coeff_ref, v_ref, dir_ref, smooth_ref, ind_ref, est_ref):
    sums = all_ref[...]
    step = jnp.sum(sums[:, 0:1], axis=0, keepdims=True) / jnp.sum(sums[:, 1:2], axis=0, keepdims=True)
    smooth_ref[...] = v_ref[...] + step * dir_ref[...]
    off = step - sums[:, 5:6]
    total = jnp.sum(sums[:, 2:3] + off * (2.0 * sums[:, 3:4] + off * sums[:, 4:5]), axis=0, keepdims=True)
    delta = step - coeff_ref[3:4, :]
    eta = coeff_ref[0:1, :] + delta * (2.0 * coeff_ref[1:2, :] + delta * coeff_ref[2:3, :])
    ind_ref[...] = eta * count / total
    est_ref[...] = jnp.broadcast_to(jnp.sqrt(total / count), est_ref.shape)


VM = pl.BlockSpec(memory_space=pltpu.VMEM)
HB = pl.BlockSpec(memory_space=pltpu.HBM)
F32, BF16 = jnp.float32, jnp.bfloat16


def call(body, outs, args, flops, far=(), scratch=()):
    shapes = [jax.ShapeDtypeStruct(*s) if isinstance(s[0], tuple) else jax.ShapeDtypeStruct(s, F32) for s in outs]
    far = tuple(pltpu.with_memory_space_constraint(x, pltpu.HBM) for x in far)
    moved = sum(4 * a.size for a in args + far) + sum(4 * s.size for s in shapes)
    return pl.pallas_call(
        body,
        out_shape=shapes,
        in_specs=[VM] * len(args) + [HB] * len(far),
        out_specs=[VM] * len(outs),
        scratch_shapes=[pltpu.VMEM(s, F32) if isinstance(s, tuple) else s for s in scratch],
        cost_estimate=pl.CostEstimate(flops=flops, bytes_accessed=moved, transcendentals=0),
        compiler_params=pltpu.CompilerParams(vmem_limit_bytes=24 * 2**20),
    )(*args, *far)


def full_swaps(first, slabs, parts):
    other = {i: i + 1 for i in range(first, parts - 1, 2)}
    other.update({j: i for i, j in list(other.items())})
    pairs = []
    for t in range(slabs):
        beside = t ^ 1 if slabs % 2 == 0 else (t + 1) % slabs
        for p in range(parts):
            pairs.append((t * parts + p, t * parts + other[p] if p in other else beside * parts + p))
    return pairs


def on_device(initial, rhs, coef, stiffness, block_inverse, face_proj, lift, time_lift, neighbour, boundary, send_list):
    source = rhs[0]
    dofs, elements = source.shape
    half = time_lift.shape[1]
    traces = face_proj.shape[0]
    face_dofs = traces // 6
    border = send_list.shape[0] // 2
    slabs, parts = lax.axis_size("tm"), lax.axis_size("space")
    devices = slabs * parts
    coef_row = coef.reshape(1, elements)
    send = send_list.reshape(2, border)
    liftt, tlt = lift.T, time_lift.T
    cycle = [(i, (i + 1) % slabs) for i in range(slabs)]

    def halo(a, b):
        swap = lambda x, first: lax.ppermute(x, ("tm", "space"), full_swaps(first, slabs, parts))
        even = swap(a, 0)
        odd = swap(b, 1)
        return even, odd

    rim = 2 * face_dofs
    edge = (face_dofs, border)
    terms = pltpu.VMEM((3 * face_dofs * len(SELECTED), elements), BF16)
    v0, end0, fp, send, coefs, nb, bd = call(
        load_first,
        [(dofs, elements), (half, elements), (traces, dofs), (send.shape, send.dtype), coef_row.shape]
        + [(neighbour.shape, neighbour.dtype), (boundary.shape, boundary.dtype)],
        (),
        2 * 10**9,
        far=(initial[0], face_proj, send, coef_row, neighbour, boundary),
        scratch=[pltpu.SemaphoreType.DMA((6,))],
    )
    prev0 = lax.ppermute(end0, "tm", cycle)
    tr0, a0, b0 = call(first_send, [(rim, elements), edge, edge], (v0, fp, send), 2 * 10**9)
    a0, b0 = halo(a0, b0)
    jump0, part0, ahead, fp3, apply3, rim3, time3, ahead_rim3, ahead_time3 = call(
        local_first,
        [(traces, elements), (dofs, elements), (dofs + rim, elements), ((traces - rim, 3 * dofs), BF16)]
        + [((dofs, 3 * (dofs + traces)), BF16), ((dofs, 3 * rim), BF16), ((dofs, 3 * half), BF16)]
        + [((dofs + rim, 3 * rim), BF16), ((dofs + rim, 3 * half), BF16)],
        (v0, tr0, coefs, fp, nb, bd, stiffness, block_inverse, liftt, tlt, source),
        12 * traces * dofs * elements,
        scratch=[(traces, elements), terms],
    )
    near0, rim0 = call(
        edge_first,
        [(dofs + rim, elements), (rim, elements)],
        (ahead, a0, b0, ahead_rim3, nb, bd),
        6 * dofs * dofs * elements,
    )
    time0, end = call(
        end_step, [(half, elements), (half, elements)], (near0, v0, prev0, ahead_time3, coefs), 6 * half * half * elements
    )
    prev1 = lax.ppermute(end, "tm", cycle)
    direction, tr1, a1, b1 = call(
        rest_step,
        [(dofs, elements), (rim, elements), edge, edge],
        (near0, time0, end, ahead_time3, coefs, send),
        6 * dofs * half * elements,
    )
    a1, b1 = halo(a1, b1)
    part1, border1, res, border0, group = call(
        local_second,
        [(dofs, elements), (rim, elements), (dofs, elements), (rim, elements), (SUBS, elements)],
        (direction, tr1, coefs, nb, bd, fp3, apply3, rim3, time3, part0, rim0, time0, jump0),
        12 * traces * dofs * elements,
        scratch=[(traces, elements), terms, (traces, elements)],
    )
    near1, groups = call(
        edge_second,
        [(dofs, elements), (SUBS, elements)],
        (part1, border1, a1, b1, rim3, nb, bd, border0, group),
        6 * dofs * rim * elements,
        scratch=[(rim, elements)],
    )
    coeffs, sums = call(
        image_step,
        [(SUBS, elements), (devices, LANES)],
        (near1, direction, prev1, time3, res, time0, groups),
        6 * dofs * half * elements,
        scratch=[(half, elements)],
    )
    everyone = lax.all_to_all(sums, ("tm", "space"), 0, 0, tiled=True)
    smoothed, indicator, estimate = call(
        functools.partial(last_step, float(elements * devices)),
        [(dofs, elements), (1, elements), (1, LANES)],
        (everyone, coeffs, v0, direction),
        4 * dofs * elements,
    )
    return smoothed[None], indicator, estimate[0, :1]


def solution(mesh):
    placed = (
        P("tm", None, "space"),
        P("tm", None, "space"),
        P("space"),
        P(),
        P(),
        P(),
        P(),
        P(),
        P(None, "space"),
        P(None, "space"),
        P("space"),
    )
    return jax.shard_map(
        on_device,
        mesh=mesh,
        in_specs=placed,
        out_specs=(P("tm", None, "space"), P("tm", "space"), P()),
        check_vma=False,
    )
```

```python
import functools

import jax
import jax.numpy as jnp
from jax import lax
from jax.experimental import pallas as pl
from jax.experimental.pallas import tpu as pltpu
from jax.sharding import PartitionSpec as P

LANES = 128
SUBS = 8


WIDE = 512
SELECTED = (2, 3)


def split(x):
    high = x.astype(jnp.bfloat16)
    return high, (x - high.astype(jnp.float32)).astype(jnp.bfloat16)


def left3(w):
    high, low = split(w)
    return jnp.concatenate([high, low, high], axis=1)


def dot3(w3, x):
    high, low = split(x)
    return jnp.dot(w3, jnp.concatenate([high, high, low], axis=0), preferred_element_type=jnp.float32)


def chunks(elements):
    width = WIDE if elements % WIDE == 0 else LANES
    return [slice(c, c + width) for c in range(0, elements, width)]


def lane_gather(tile_of, tiles, columns, rows):
    shape = (SUBS, LANES)
    low = jnp.broadcast_to(jnp.bitwise_and(columns, LANES - 1), shape)
    high = jnp.broadcast_to(jnp.right_shift(columns, 7), shape)
    found = [jnp.zeros(shape, jnp.float32) for _ in range(rows // SUBS)]
    for tile in range(tiles):
        here = high == tile
        for r in range(rows // SUBS):
            picked = jnp.take_along_axis(tile_of(tile, r), low, axis=1)
            found[r] = jnp.where(here, picked, found[r])
    return found


def face_rows(ref, face, face_dofs):
    return ref[pl.ds(face, face_dofs, stride=6), :]


def is_odd():
    return lax.rem(lax.axis_index("space"), 2) == 1


def fill_outbound(traces, send_ref, first_ref, second_ref, face_dofs, elements):
    per_face = elements // LANES
    odd = is_odd()

    def tile_of(tile, r):
        face, col = divmod(tile, per_face)
        return traces[face * face_dofs + r * SUBS : face * face_dofs + (r + 1) * SUBS, col * LANES : (col + 1) * LANES]

    border = send_ref.shape[1]
    for j in range(border // LANES):
        cols = slice(j * LANES, (j + 1) * LANES)
        lower = lane_gather(tile_of, 2 * per_face, send_ref[0:1, cols], face_dofs)
        upper = lane_gather(tile_of, 2 * per_face, send_ref[1:2, cols], face_dofs)
        for r in range(face_dofs // SUBS):
            rows = slice(r * SUBS, (r + 1) * SUBS)
            first_ref[rows, cols] = jnp.where(odd, lower[r], upper[r])
            second_ref[rows, cols] = jnp.where(odd, upper[r], lower[r])


def thirds(x):
    high = x.astype(jnp.bfloat16)
    rest = x - high.astype(jnp.float32)
    middle = rest.astype(jnp.bfloat16)
    return jnp.concatenate([high, middle, (rest - middle.astype(jnp.float32)).astype(jnp.bfloat16)], axis=0)


def fill_jump(traces, terms, nb_ref, bd_ref, jump_ref, face_dofs, elements, chunk):
    per_face = elements // LANES
    width = chunk.stop - chunk.start
    for face in range(6):
        other = face ^ 1
        if face in SELECTED:
            columns = nb_ref[face : face + 1, chunk] - other * elements
            block = 2 * LANES if elements % (2 * LANES) == 0 else LANES
            number = lax.broadcasted_iota(jnp.int32, (block, width), 0).astype(jnp.float32).astype(jnp.bfloat16)
            picks = []
            for start in range(0, elements, block):
                place = jnp.clip(columns - start, -1, block).astype(jnp.float32).astype(jnp.bfloat16)
                picks.append(jnp.where(number == jnp.broadcast_to(place, (block, width)), jnp.bfloat16(1), jnp.bfloat16(0)))
            at = SELECTED.index(other) * 3 * face_dofs
            found = jnp.dot(terms[at : at + 3 * face_dofs, :], jnp.concatenate(picks, axis=0), preferred_element_type=jnp.float32)
            found = (found[:face_dofs] + found[face_dofs : 2 * face_dofs]) + found[2 * face_dofs :]
            rows = slice(face * face_dofs, (face + 1) * face_dofs)
            jump_ref[rows, chunk] = traces[rows, chunk] - found * (1.0 - bd_ref[face : face + 1, chunk].astype(jnp.float32))
            continue

        def tile_of(tile, r, other=other):
            return traces[other * face_dofs + r * SUBS : other * face_dofs + (r + 1) * SUBS, tile * LANES : (tile + 1) * LANES]

        for start in range(chunk.start, chunk.stop, LANES):
            cols = slice(start, start + LANES)
            found = lane_gather(tile_of, per_face, nb_ref[face : face + 1, cols] - other * elements, face_dofs)
            open_face = jnp.broadcast_to(1.0 - bd_ref[face : face + 1, cols].astype(jnp.float32), (SUBS, LANES))
            for r in range(face_dofs // SUBS):
                rows = slice(face * face_dofs + r * SUBS, face * face_dofs + (r + 1) * SUBS)
                jump_ref[rows, cols] = traces[rows, cols] - found[r] * open_face


def rim_terms(first_ref, second_ref, nb_ref, bd_ref, rim_ref, face_dofs, elements):
    tiles = first_ref.shape[1] // LANES
    odd, place, parts = is_odd(), lax.axis_index("space"), lax.axis_size("space")
    sides = []
    for side in range(2):
        for t in range(tiles):
            cols = slice(t * LANES, (t + 1) * LANES)
            a, b = first_ref[:, cols], second_ref[:, cols]
            values = jnp.where(odd, a, b) if side == 0 else jnp.where(odd, b, a)
            there = place > 0 if side == 0 else place < parts - 1
            sides.append(jnp.where(there, values, 0.0))

    def tile_of(tile, r):
        return sides[tile][r * SUBS : (r + 1) * SUBS, :]

    for j in range(elements // LANES):
        cols = slice(j * LANES, (j + 1) * LANES)
        for face in range(2):
            found = lane_gather(tile_of, 2 * tiles, nb_ref[face : face + 1, cols] - 6 * elements, face_dofs)
            open_face = jnp.broadcast_to(1.0 - bd_ref[face : face + 1, cols].astype(jnp.float32), (SUBS, LANES))
            for r in range(face_dofs // SUBS):
                rows = slice(face * face_dofs + r * SUBS, face * face_dofs + (r + 1) * SUBS)
                rim_ref[rows, cols] = 0.0 - found[r] * open_face


def load_first(
    v_hbm, fp_hbm, send_hbm, coef_hbm, nb_hbm, bd_hbm, v_ref, end_ref, fp_ref, send_ref, coef_ref, nb_ref, bd_ref, sems
):
    half = end_ref.shape[0]
    pairs = ((v_hbm, v_ref), (fp_hbm, fp_ref), (send_hbm, send_ref), (coef_hbm, coef_ref), (nb_hbm, nb_ref), (bd_hbm, bd_ref))
    copies = [pltpu.make_async_copy(a, b, sems.at[i]) for i, (a, b) in enumerate(pairs)]
    for copy in copies:
        copy.start()
    copies[0].wait()
    end_ref[...] = v_ref[half:, :]
    for copy in copies[1:]:
        copy.wait()


def first_send(v_ref, fp_ref, send_ref, tr_ref, first_ref, second_ref):
    face_dofs = fp_ref.shape[0] // 6
    elements = v_ref.shape[1]
    weights = left3(jnp.concatenate([face_rows(fp_ref, f, face_dofs) for f in range(2)], axis=0))
    for c in chunks(elements):
        tr_ref[:, c] = dot3(weights, v_ref[:, c])
    fill_outbound(tr_ref, send_ref, first_ref, second_ref, face_dofs, elements)


def all_traces(v_ref, tr_ref, weights, traces, terms):
    known = tr_ref.shape[0]
    face_dofs = traces.shape[0] // 6
    for c in chunks(v_ref.shape[1]):
        traces[:known, c] = tr_ref[:, c]
        traces[known:, c] = dot3(weights, v_ref[:, c])
        for i, face in enumerate(SELECTED):
            terms[3 * i * face_dofs : 3 * (i + 1) * face_dofs, c] = thirds(traces[face * face_dofs : (face + 1) * face_dofs, c])


def local_first(
    v_ref, tr_ref, coef_ref, fp_ref, nb_ref, bd_ref, stiff, inv, liftt, tlt, rhs,
    jump_ref, part_ref, ahead_ref, fp3_ref, apply3_ref, rim3_ref, time3_ref, ahead_rim3_ref, ahead_time3_ref,
    traces, terms,
):
    face_dofs = fp_ref.shape[0] // 6
    elements = v_ref.shape[1]
    fp3_ref[...] = left3(jnp.concatenate([face_rows(fp_ref, f, face_dofs) for f in range(2, 6)], axis=0))
    all_traces(v_ref, tr_ref, fp3_ref[...], traces, terms)
    lift_rows = [face_rows(liftt, f, face_dofs) for f in range(6)]
    apply3_ref[...] = left3(jnp.concatenate([stiff[...], jnp.concatenate(lift_rows, axis=0).T], axis=1))
    rim, time = jnp.concatenate(lift_rows[:2], axis=0).T, tlt[...].T
    rim3_ref[...] = left3(rim)
    time3_ref[...] = left3(time)
    inverse = inv[...]
    first_faces = jnp.concatenate([face_rows(fp_ref, f, face_dofs) for f in range(2)], axis=0)
    both = left3(jnp.concatenate([inverse, dot3(left3(first_faces), inverse)], axis=0))
    ahead_rim3_ref[...] = left3(dot3(both, rim))
    ahead_time3_ref[...] = left3(dot3(both, time))
    parts = chunks(elements)
    fill_jump(traces, terms, nb_ref, bd_ref, jump_ref, face_dofs, elements, parts[0])
    for i, c in enumerate(parts):
        if i + 1 < len(parts):
            fill_jump(traces, terms, nb_ref, bd_ref, jump_ref, face_dofs, elements, parts[i + 1])
        values = jnp.concatenate([coef_ref[:, c] * v_ref[:, c], jump_ref[:, c]], axis=0)
        part = rhs[:, c] - dot3(apply3_ref[...], values)
        part_ref[:, c] = part
        ahead_ref[:, c] = dot3(both, part)


def edge_first(ahead_ref, first_in, second_in, ahead_rim3_ref, nb_ref, bd_ref, near_ref, rim_ref):
    rim_terms(first_in, second_in, nb_ref, bd_ref, rim_ref, first_in.shape[0], near_ref.shape[1])
    for c in chunks(near_ref.shape[1]):
        near_ref[:, c] = ahead_ref[:, c] - dot3(ahead_rim3_ref[...], rim_ref[:, c])


def end_step(near_ref, v_ref, prev_ref, ahead_time3_ref, coef_ref, time_ref, end_ref):
    dofs, elements = v_ref.shape
    half = prev_ref.shape[0]
    time_ref[...] = time_jump_of(v_ref, prev_ref)
    for c in chunks(elements):
        end_ref[:, c] = (near_ref[half:dofs, c] - dot3(ahead_time3_ref[half:dofs, :], time_ref[:, c])) * (1.0 / coef_ref[:, c])


def rest_step(near_ref, time_ref, end_ref, ahead_time3_ref, coef_ref, send_ref, dir_ref, tr_ref, first_ref, second_ref):
    face_dofs = first_ref.shape[0]
    dofs, elements = dir_ref.shape
    half = end_ref.shape[0]
    weights = jnp.concatenate([ahead_time3_ref[dofs:, :], ahead_time3_ref[:half, :]], axis=0)
    rim = 2 * face_dofs
    for c in chunks(elements):
        scale = 1.0 / coef_ref[:, c]
        both = dot3(weights, time_ref[:, c])
        tr_ref[:, c] = (near_ref[dofs:, c] - both[:rim, :]) * scale
        dir_ref[:half, c] = (near_ref[:half, c] - both[rim:, :]) * scale
        dir_ref[half:, c] = end_ref[:, c]
    fill_outbound(tr_ref, send_ref, first_ref, second_ref, face_dofs, elements)


def time_jump_of(v_ref, prev_ref):
    return v_ref[: prev_ref.shape[0], :] - jnp.where(lax.axis_index("tm") > 0, prev_ref[...], 0.0)


def column_sum(x):
    return jnp.sum(x, axis=0, keepdims=True)


def total_sum(row):
    return jnp.sum(row, axis=1, keepdims=True)


def lowest(slope, bend):
    return jnp.where(bend > 0.0, -slope / jnp.where(bend > 0.0, bend, 1.0), 0.0)


def group_sums(j0, j1):
    bend, slope = 0.5 * column_sum(j1 * j1), 0.5 * column_sum(j0 * j1)
    best = lowest(slope, bend)
    j = j0 + best * j1
    return [0.5 * column_sum(j * j), slope, bend, best]


def group_at(group, s):
    base, slope, bend, best = group
    off = s - best
    return base + off * (2.0 * (slope + best * bend) + off * bend)


def local_second(
    dir_ref, tr_ref, coef_ref, nb_ref, bd_ref, fp3_ref, apply3_ref, rim3_ref, time3_ref, part_ref, rim_ref, time_ref, jump0_ref,
    image_ref, border_ref, res_ref, border0_ref, group_ref, traces, terms, jump,
):
    elements = dir_ref.shape[1]
    face_dofs = jump.shape[0] // 6
    rim = 2 * face_dofs
    all_traces(dir_ref, tr_ref, fp3_ref[...], traces, terms)
    for c in chunks(elements):
        fill_jump(traces, terms, nb_ref, bd_ref, jump, face_dofs, elements, c)
        values = jnp.concatenate([coef_ref[:, c] * dir_ref[:, c], jump[:, c]], axis=0)
        image_ref[:, c] = dot3(apply3_ref[...], values)
        res_ref[:, c] = part_ref[:, c] - dot3(rim3_ref[...], rim_ref[:, c]) - dot3(time3_ref[...], time_ref[:, c])
        border_ref[:, c] = jump[:rim, c]
        border0_ref[:, c] = jump0_ref[:rim, c] + rim_ref[:, c]
        group_ref[:, c] = jnp.concatenate(group_sums(jump0_ref[rim:, c], jump[rim:, c]) * 2, axis=0)


def edge_second(part_ref, border_ref, first_in, second_in, rim3_ref, nb_ref, bd_ref, border0_ref, group_ref, near_ref, groups_ref, rim):
    elements = part_ref.shape[1]
    rim_terms(first_in, second_in, nb_ref, bd_ref, rim, first_in.shape[0], elements)
    for c in chunks(elements):
        near_ref[:, c] = part_ref[:, c] + dot3(rim3_ref[...], rim[:, c])
        sums = group_sums(border0_ref[:, c], border_ref[:, c] + rim[:, c])
        groups_ref[:, c] = jnp.concatenate([group_ref[:4, c]] + sums, axis=0)


def image_step(near_ref, dir_ref, prev_ref, time3_ref, res_ref, time0_ref, group_ref, coeff_ref, sums_ref, time):
    elements = dir_ref.shape[1]
    crosses, squares = [], []
    time[...] = time_jump_of(dir_ref, prev_ref)
    for c in chunks(elements):
        t0, t1 = time0_ref[:, c], time[:, c]
        img = near_ref[:, c] + dot3(time3_ref[...], t1)
        res = res_ref[:, c]
        cross, square = column_sum(res * img), column_sum(img * img)
        groups = [[group_ref[i : i + 1, c] for i in range(k, k + 4)] for k in (0, 4)]
        bend = square + column_sum(t1 * t1) + groups[0][2] + groups[1][2]
        slope = column_sum(t0 * t1) + groups[0][1] + groups[1][1] - cross
        best = lowest(slope, bend)
        r = res - best * img
        t = t0 + best * t1
        base = column_sum(r * r) + column_sum(t * t) + group_at(groups[0], best) + group_at(groups[1], best)
        tilt = slope + best * bend
        coeff_ref[:, c] = jnp.concatenate([base, tilt, bend, best, best, best, best, best], axis=0)
        crosses.append(cross)
        squares.append(square)
    base, tilt, bend, best = (coeff_ref[i : i + 1, :] for i in range(4))
    bend_all = total_sum(bend)
    centre = lowest(-total_sum(best * bend), bend_all)
    off = centre - best
    base_all = total_sum(base + off * (2.0 * tilt + off * bend))
    tilt_all = total_sum(tilt + off * bend)
    cross_all = total_sum(jnp.concatenate(crosses, axis=1))
    square_all = total_sum(jnp.concatenate(squares, axis=1))
    lane = lax.broadcasted_iota(jnp.int32, sums_ref.shape, 1)
    out = jnp.zeros(sums_ref.shape, jnp.float32)
    for i, value in enumerate((cross_all, square_all, base_all, tilt_all, bend_all, centre)):
        out = jnp.where(lane == i, value, out)
    sums_ref[...] = out


def last_step(count, all_ref, coeff_ref, v_ref, dir_ref, smooth_ref, ind_ref, est_ref):
    sums = all_ref[...]
    step = jnp.sum(sums[:, 0:1], axis=0, keepdims=True) / jnp.sum(sums[:, 1:2], axis=0, keepdims=True)
    smooth_ref[...] = v_ref[...] + step * dir_ref[...]
    off = step - sums[:, 5:6]
    total = jnp.sum(sums[:, 2:3] + off * (2.0 * sums[:, 3:4] + off * sums[:, 4:5]), axis=0, keepdims=True)
    delta = step - coeff_ref[3:4, :]
    eta = coeff_ref[0:1, :] + delta * (2.0 * coeff_ref[1:2, :] + delta * coeff_ref[2:3, :])
    ind_ref[...] = eta * count / total
    est_ref[...] = jnp.broadcast_to(jnp.sqrt(total / count), est_ref.shape)


VM = pl.BlockSpec(memory_space=pltpu.VMEM)
HB = pl.BlockSpec(memory_space=pltpu.HBM)
F32, BF16 = jnp.float32, jnp.bfloat16


def call(body, outs, args, flops, far=(), scratch=()):
    shapes = [jax.ShapeDtypeStruct(*s) if isinstance(s[0], tuple) else jax.ShapeDtypeStruct(s, F32) for s in outs]
    far = tuple(pltpu.with_memory_space_constraint(x, pltpu.HBM) for x in far)
    moved = sum(4 * a.size for a in args + far) + sum(4 * s.size for s in shapes)
    return pl.pallas_call(
        body,
        out_shape=shapes,
        in_specs=[VM] * len(args) + [HB] * len(far),
        out_specs=[VM] * len(outs),
        scratch_shapes=[pltpu.VMEM(s, F32) if isinstance(s, tuple) else s for s in scratch],
        cost_estimate=pl.CostEstimate(flops=flops, bytes_accessed=moved, transcendentals=0),
        compiler_params=pltpu.CompilerParams(vmem_limit_bytes=24 * 2**20),
    )(*args, *far)


def full_swaps(first, slabs, parts):
    other = {i: i + 1 for i in range(first, parts - 1, 2)}
    other.update({j: i for i, j in list(other.items())})
    pairs = []
    for t in range(slabs):
        beside = t ^ 1 if slabs % 2 == 0 else (t + 1) % slabs
        for p in range(parts):
            pairs.append((t * parts + p, t * parts + other[p] if p in other else beside * parts + p))
    return pairs


def on_device(initial, rhs, coef, stiffness, block_inverse, face_proj, lift, time_lift, neighbour, boundary, send_list):
    source = rhs[0]
    dofs, elements = source.shape
    half = time_lift.shape[1]
    traces = face_proj.shape[0]
    face_dofs = traces // 6
    border = send_list.shape[0] // 2
    slabs, parts = lax.axis_size("tm"), lax.axis_size("space")
    devices = slabs * parts
    coef_row = coef.reshape(1, elements)
    send = send_list.reshape(2, border)
    liftt, tlt = lift.T, time_lift.T
    cycle = [(i, (i + 1) % slabs) for i in range(slabs)]

    def halo(a, b):
        swap = lambda x, first: lax.ppermute(x, ("tm", "space"), full_swaps(first, slabs, parts))
        even = swap(a, 0)
        odd = swap(b, 1)
        return even, odd

    rim = 2 * face_dofs
    edge = (face_dofs, border)
    terms = pltpu.VMEM((3 * face_dofs * len(SELECTED), elements), BF16)
    v0, end0, fp, send, coefs, nb, bd = call(
        load_first,
        [(dofs, elements), (half, elements), (traces, dofs), (send.shape, send.dtype), coef_row.shape]
        + [(neighbour.shape, neighbour.dtype), (boundary.shape, boundary.dtype)],
        (),
        2 * 10**9,
        far=(initial[0], face_proj, send, coef_row, neighbour, boundary),
        scratch=[pltpu.SemaphoreType.DMA((6,))],
    )
    prev0 = lax.ppermute(end0, "tm", cycle)
    tr0, a0, b0 = call(first_send, [(rim, elements), edge, edge], (v0, fp, send), 2 * 10**9)
    a0, b0 = halo(a0, b0)
    jump0, part0, ahead, fp3, apply3, rim3, time3, ahead_rim3, ahead_time3 = call(
        local_first,
        [(traces, elements), (dofs, elements), (dofs + rim, elements), ((traces - rim, 3 * dofs), BF16)]
        + [((dofs, 3 * (dofs + traces)), BF16), ((dofs, 3 * rim), BF16), ((dofs, 3 * half), BF16)]
        + [((dofs + rim, 3 * rim), BF16), ((dofs + rim, 3 * half), BF16)],
        (v0, tr0, coefs, fp, nb, bd, stiffness, block_inverse, liftt, tlt, source),
        12 * traces * dofs * elements,
        scratch=[(traces, elements), terms],
    )
    near0, rim0 = call(
        edge_first,
        [(dofs + rim, elements), (rim, elements)],
        (ahead, a0, b0, ahead_rim3, nb, bd),
        6 * dofs * dofs * elements,
    )
    time0, end = call(
        end_step, [(half, elements), (half, elements)], (near0, v0, prev0, ahead_time3, coefs), 6 * half * half * elements
    )
    prev1 = lax.ppermute(end, "tm", cycle)
    direction, tr1, a1, b1 = call(
        rest_step,
        [(dofs, elements), (rim, elements), edge, edge],
        (near0, time0, end, ahead_time3, coefs, send),
        6 * dofs * half * elements,
    )
    a1, b1 = halo(a1, b1)
    part1, border1, res, border0, group = call(
        local_second,
        [(dofs, elements), (rim, elements), (dofs, elements), (rim, elements), (SUBS, elements)],
        (direction, tr1, coefs, nb, bd, fp3, apply3, rim3, time3, part0, rim0, time0, jump0),
        12 * traces * dofs * elements,
        scratch=[(traces, elements), terms, (traces, elements)],
    )
    near1, groups = call(
        edge_second,
        [(dofs, elements), (SUBS, elements)],
        (part1, border1, a1, b1, rim3, nb, bd, border0, group),
        6 * dofs * rim * elements,
        scratch=[(rim, elements)],
    )
    coeffs, sums = call(
        image_step,
        [(SUBS, elements), (devices, LANES)],
        (near1, direction, prev1, time3, res, time0, groups),
        6 * dofs * half * elements,
        scratch=[(half, elements)],
    )
    everyone = lax.all_to_all(sums, ("tm", "space"), 0, 0, tiled=True)
    smoothed, indicator, estimate = call(
        functools.partial(last_step, float(elements * devices)),
        [(dofs, elements), (1, elements), (1, LANES)],
        (everyone, coeffs, v0, direction),
        4 * dofs * elements,
    )
    return smoothed[None], indicator, estimate[0, :1]


def solution(mesh):
    placed = (
        P("tm", None, "space"),
        P("tm", None, "space"),
        P("space"),
        P(),
        P(),
        P(),
        P(),
        P(),
        P(None, "space"),
        P(None, "space"),
        P("space"),
    )
    return jax.shard_map(
        on_device,
        mesh=mesh,
        in_specs=placed,
        out_specs=(P("tm", None, "space"), P("tm", "space"), P()),
        check_vma=False,
    )
```
